32 devices in a mesh: seq: 8 (over y, x, core), chan: 4 (over z).
Axes of the slice: x: 2, y: 2, z: 4, core: 2. Of those that a mesh axis runs over, the one named last changes fastest.
Arguments:
- values_in: bfloat16 [4096, 1024], P(('seq', 'chan')), may hold values from -6 to 6
- gate_in: bfloat16 [4096, 1024], P(('seq', 'chan')), may hold values from -6 to 6
- gate_out: bfloat16 [4096, 1024], P(('seq', 'chan')), may hold values from -6 to 6
- cotangent: bfloat16 [4096, 1024], P(('seq', 'chan')), may hold values from -6 to 6
- filter_spectra: float32 [2, 8, 2, 512, 1024], P(None, 'seq', None, None, 'chan'), may hold values from -4 to 4, as said below
Outputs:
- output: bfloat16 [4096, 1024], P(('seq', 'chan'))
- grad_values: bfloat16 [4096, 1024], P(('seq', 'chan'))
- grad_gate_in: bfloat16 [4096, 1024], P(('seq', 'chan'))
- grad_gate_out: bfloat16 [4096, 1024], P(('seq', 'chan'))
- grad_filter: float32 [2, 8, 2, 512, 1024], P(None, 'seq', None, None, 'chan')
The draws below stay inside these ranges and needn't reach their ends.
Inputs may be any that keep to these rules, and one draw needn't show every extreme that they name: `filter_spectra`: the spectrum is that of a real filter: the value at frequency 8192 - f is the complex conjugate of the value at f, and the values at frequencies 0 and 4096 are real.
All inputs are finite; a program needn't handle non-finite values.
Results may differ from the reference program's by a relative error of at most 0.001.
Values may be sent and summed in bfloat16 or wider, within the bound.
A program may use at most 128 MiB of HBM per device.

```python
import jax
import jax.numpy as jnp
import numpy as np
from jax import lax

D = 1024
TOK_DEV = 512
SHARDS = 8
SEQ = 4096
NFFT = 8192


def layout_frequencies_drawn():
    bit_count = SHARDS.bit_length() - 1
    mirror_table = np.zeros(SHARDS, np.int64)
    for number in range(SHARDS):
        result = 0
        for bit_place in range(bit_count):
            if number >> bit_place & 1:
                result = result | 1 << bit_count - 1 - bit_place
        mirror_table[number] = result
    shard_ids = np.arange(SHARDS)[:, None, None]
    parity = np.arange(2)[None, :, None]
    column = np.arange(TOK_DEV)[None, None, :]
    frequency = 2 * mirror_table[shard_ids] + parity + 2 * SHARDS * column
    return frequency.reshape(-1)


def draw_filter_spectra(key, part):
    total = 2 * TOK_DEV * SHARDS
    key_real = jax.random.fold_in(key, 101)
    key_imag = jax.random.fold_in(key, 202)
    real_part = jnp.clip(jax.random.normal(key_real, (total, D), jnp.float32), -4.0, 4.0)
    imag_part = jnp.clip(jax.random.normal(key_imag, (total, D), jnp.float32), -4.0, 4.0)
    mirrored = (total - jnp.arange(total, dtype=jnp.int32)) % total
    herm_real = 0.5 * (real_part + jnp.take(real_part, mirrored, axis=0))
    herm_imag = 0.5 * (imag_part - jnp.take(imag_part, mirrored, axis=0))
    ordering = jnp.asarray(layout_frequencies_drawn().astype(np.int32))
    layout_real = jnp.take(herm_real, ordering, axis=0).reshape(SHARDS, 2, TOK_DEV, D)
    layout_imag = jnp.take(herm_imag, ordering, axis=0).reshape(SHARDS, 2, TOK_DEV, D)
    return jnp.stack([layout_real, layout_imag]).astype(jnp.float32)


def shard_levels(stream_key, extent, shards, least, largest):
    factor_of, own = 1.0, jax.random.fold_in(stream_key, 6)
    for position, shards_of in shards:
        heights = jnp.exp(jax.random.uniform(jax.random.fold_in(own, position), (shards_of,), jnp.float32, least / len(shards), largest / len(shards)))
        factor_of = factor_of * jnp.repeat(heights, extent[position] // shards_of).reshape([-1 if axis == position else 1 for axis in range(len(extent))])
    return factor_of


def gaussian(stream_key, dims, width, reach, pieces=(), held_as=jnp.bfloat16):
    loudness = shard_levels(stream_key, dims, pieces, -0.22, 0.18) if pieces else 1.0
    entries = jax.random.normal(stream_key, dims, jnp.float32) * width * loudness
    return jnp.minimum(jnp.maximum(entries, -reach), reach).astype(held_as)


def setup_inputs(seed: int = 0) -> dict:
    key_list = jax.random.split(jax.random.key(seed), 6)
    return {
        "values_in": gaussian(key_list[0], (SEQ, D), 1.0, 6.0, ((0, 32),)),
        "gate_in": gaussian(key_list[1], (SEQ, D), 1.0, 6.0, ((0, 32),)),
        "gate_out": gaussian(key_list[2], (SEQ, D), 1.0, 6.0, ((0, 32),)),
        "cotangent": gaussian(key_list[3], (SEQ, D), 1.0, 6.0, ((0, 32),)),
        "filter_spectra": draw_filter_spectra(jax.random.fold_in(key_list[5], 71), 0),
    }


def layout_frequencies():
    bit_count = SHARDS.bit_length() - 1
    mirror_table = np.zeros(SHARDS, np.int64)
    for number in range(SHARDS):
        result = 0
        for bit_place in range(bit_count):
            if (number >> bit_place) & 1:
                result = result | (1 << (bit_count - 1 - bit_place))
        mirror_table[number] = result
    shard_ids = np.arange(SHARDS)[:, None, None]
    parity = np.arange(2)[None, :, None]
    column = np.arange(TOK_DEV)[None, None, :]
    frequency = 2 * mirror_table[shard_ids] + parity + 2 * SHARDS * column
    return frequency.reshape(-1)


def reference(values_in, gate_in, gate_out, cotangent, filter_spectra):
    frequency = layout_frequencies()
    to_natural = jnp.asarray(np.argsort(frequency).astype(np.int32))
    to_layout = jnp.asarray(frequency.astype(np.int32))
    flat_re = filter_spectra[0].reshape(SHARDS * 2 * TOK_DEV, D)
    flat_im = filter_spectra[1].reshape(SHARDS * 2 * TOK_DEV, D)
    spectrum = lax.complex(jnp.take(flat_re, to_natural, axis=0), jnp.take(flat_im, to_natural, axis=0))
    signal = values_in.astype(jnp.float32) * gate_in.astype(jnp.float32)
    carried = cotangent.astype(jnp.float32) * gate_out.astype(jnp.float32)
    padding = ((0, SEQ), (0, 0))
    spec_signal = jnp.fft.fft(jnp.pad(signal, padding), axis=0)
    spec_carried = jnp.fft.fft(jnp.pad(carried, padding), axis=0)
    conv = jnp.real(jnp.fft.ifft(spec_signal * spectrum, axis=0))[:SEQ]
    back = jnp.real(jnp.fft.ifft(jnp.conj(spectrum) * spec_carried, axis=0))[:SEQ]
    output = (gate_out.astype(jnp.float32) * conv).astype(jnp.bfloat16)
    grad_gate_out = (cotangent.astype(jnp.float32) * conv).astype(jnp.bfloat16)
    grad_values = (back * gate_in.astype(jnp.float32)).astype(jnp.bfloat16)
    grad_gate_in = (back * values_in.astype(jnp.float32)).astype(jnp.bfloat16)
    product = jnp.conj(spec_signal) * spec_carried / NFFT
    grad_re = jnp.take(jnp.real(product), to_layout, axis=0).reshape(SHARDS, 2, TOK_DEV, D)
    grad_im = jnp.take(jnp.imag(product), to_layout, axis=0).reshape(SHARDS, 2, TOK_DEV, D)
    grad_filter = jnp.stack([grad_re, grad_im]).astype(jnp.float32)
    return output, grad_values, grad_gate_in, grad_gate_out, grad_filter
```

```python
import functools
import math

import jax
import jax.numpy as jnp
import numpy as np
from jax import lax
from jax.experimental import pallas as pl
from jax.experimental.pallas import tpu as pltpu
from jax.sharding import PartitionSpec as P

MESH = pl.DeviceIdType.MESH
ANY = pl.BlockSpec(memory_space=pl.ANY)
WHOLE = pl.BlockSpec(memory_space=pltpu.VMEM)
LANES = 128
STEPS = 4


def mirrored(number, bits):
    out = 0
    for place in range(bits):
        out = out + ((number >> place) & 1) * (1 << (bits - 1 - place))
    return out


def meet(peers):
    barrier = pltpu.get_barrier_semaphore()
    for peer in peers:
        pl.semaphore_signal(barrier, inc=1, device_id=peer, device_id_type=MESH)
    pl.semaphore_wait(barrier, len(peers))


def lane_group(width):
    return lax.broadcasted_iota(jnp.int32, (1, LANES), 1) // width


def swap_lanes(arrays, width):
    arrays = list(arrays)
    group = lane_group(width)
    bit = 1
    while bit < len(arrays):
        low = (group & bit) == 0
        shift = bit * width
        for i in range(len(arrays)):
            if i & bit:
                continue
            a, b = arrays[i], arrays[i | bit]
            arrays[i] = jnp.where(low, a, pltpu.roll(b, shift, 1))
            arrays[i | bit] = jnp.where(low, pltpu.roll(a, LANES - shift, 1), b)
        bit *= 2
    return arrays


def halves(data):
    high = data.astype(jnp.bfloat16)
    return high, (data - high.astype(jnp.float32)).astype(jnp.bfloat16)


def add(a, b):
    if a is None:
        return b
    return a if b is None else a + b


def sub(a, b):
    if b is None:
        return a
    return -b if a is None else a - b


def scale(a, factor):
    if a is None or abs(factor) < 1e-12:
        return None
    if abs(factor - 1.0) < 1e-12:
        return a
    return -a if abs(factor + 1.0) < 1e-12 else a * factor


def turned(value, numerator, denominator):
    angle = 2.0 * math.pi * numerator / denominator
    cos, sin = math.cos(angle), math.sin(angle)
    real, imag = value
    return (
        sub(scale(real, cos), scale(imag, sin)),
        add(scale(real, sin), scale(imag, cos)),
    )


def conjugate(value):
    return (value[0], scale(value[1], -1.0))


def forward_ladder(values):
    if len(values) == 1:
        return [(values[0], None), (values[0], None)]
    count = 2 * len(values)
    even, odd = forward_ladder(values[0::2]), forward_ladder(values[1::2])
    out = [None] * (count // 2 + 1)
    for k in range(count // 4 + 1):
        spun = turned(odd[k], -k, count)
        out[k] = (add(even[k][0], spun[0]), add(even[k][1], spun[1]))
        if k != count // 4:
            away = (sub(even[k][0], spun[0]), sub(even[k][1], spun[1]))
            out[count // 2 - k] = conjugate(away)
    return out


def inverse_ladder(values):
    if len(values) == 2:
        return [add(values[0][0], values[1][0])]
    half = len(values) - 1
    even, odd = [], []
    for k in range(half // 2):
        a, b = values[k], conjugate(values[half - k])
        even.append((add(a[0], b[0]), add(a[1], b[1])))
        odd.append(turned((sub(a[0], b[0]), sub(a[1], b[1])), k, 2 * half))
    even.append(values[half // 2])
    odd.append(turned(values[half // 2], 1, 4))
    out = [None] * half
    out[0::2], out[1::2] = inverse_ladder(even), inverse_ladder(odd)
    return out


def arrange_kernel(width, *refs):
    inputs, filt, source, hsrc, hspec = refs[:4], *refs[4:]
    fan, rows = source.shape[0], source.shape[2]
    for a in range(4):
        block = inputs[a][...].astype(jnp.float32)
        parts = [block[g * rows : (g + 1) * rows] for g in range(fan)]
        for u, part in enumerate(swap_lanes(parts, width)):
            source[u, a] = part.astype(jnp.bfloat16)
    pack = fan // 4
    span = filt.shape[3] // 2
    even = [
        filt[p, e, q, pl.ds(0, span, stride=2), :]
        for q in range(pack)
        for p in range(2)
        for e in range(2)
    ]
    for u, part in enumerate(swap_lanes(even, width)):
        hsrc[u] = part
    odd = [
        filt[p, 0, q, pl.ds(1 + half * span, span // 2, stride=2), :]
        for q in range(pack)
        for half in range(2)
        for p in range(2)
    ]
    for u, part in enumerate(swap_lanes(odd, width)):
        hspec[u] = part


def arrange(inputs, filt, devices, shards):
    rows, channels = inputs[0].shape
    width = channels // devices
    fan = LANES // width
    pack = fan // 4
    length = filt.shape[3]
    blocks = channels // LANES
    part = blocks // STEPS
    wide = length // pack
    return pl.pallas_call(
        functools.partial(arrange_kernel, width),
        grid=(blocks,),
        out_shape=(
            jax.ShapeDtypeStruct((devices, 4, rows // fan, LANES), jnp.bfloat16),
            jax.ShapeDtypeStruct((shards, wide // 2, LANES), jnp.float32),
            jax.ShapeDtypeStruct((shards, wide // 4, LANES), jnp.float32),
        ),
        in_specs=[pl.BlockSpec((rows, LANES), lambda t: (0, t))] * 4
        + [
            pl.BlockSpec(
                (2, 2, pack, wide // STEPS, LANES),
                lambda t: (0, 0, 0, t % STEPS, t // STEPS),
            )
        ],
        out_specs=(
            pl.BlockSpec((fan, 4, rows // fan, LANES), lambda t: (t, 0, 0, 0)),
            pl.BlockSpec((fan, wide // 2 // STEPS, LANES), lambda t: (t // STEPS, t % STEPS, 0)),
            pl.BlockSpec((fan, wide // 4 // STEPS, LANES), lambda t: (t // STEPS, t % STEPS, 0)),
        ),
        name="arrange",
    )(*inputs, filt.reshape(2, 2, pack, wide, filt.shape[4]))


def scatter_kernel(source, hsrc, hspec, held, hheld, special, *sems):
    own_sem, t_send, t_recv, f_send, f_recv, x_send, x_recv = sems
    groups, shards = source.shape[:2]
    s, c = lax.axis_index("seq"), lax.axis_index("chan")
    peers = [(j, d) for d in range(groups - 1, -1, -1) for j in range(shards) if j or d]
    meet([(s ^ j, c ^ d) for j, d in peers])

    def tokens(j, d, landing):
        to_s, to_c = (s ^ j, c ^ d) if landing else (s, c)
        return pltpu.make_async_remote_copy(
            src_ref=source.at[c ^ d, s ^ j],
            dst_ref=held.at[to_s, to_c],
            send_sem=t_send.at[d * shards + j],
            recv_sem=t_recv.at[d * shards + j],
            device_id=(s ^ j, c ^ d),
            device_id_type=MESH,
        )

    def spectrum(j, landing):
        return pltpu.make_async_remote_copy(
            src_ref=hsrc.at[s ^ j],
            dst_ref=hheld.at[s ^ j] if landing else hheld.at[s],
            send_sem=f_send.at[j],
            recv_sem=f_recv.at[j],
            device_id=(s ^ j, c),
            device_id_type=MESH,
        )

    def extra(j):
        return pltpu.make_async_remote_copy(
            src_ref=hspec.at[j],
            dst_ref=special,
            send_sem=x_send.at[j],
            recv_sem=x_recv,
            device_id=(j, c),
            device_id_type=MESH,
        )

    for j, d in peers:
        tokens(j, d, False).start()
    for j in range(1, shards):
        spectrum(j, False).start()

    @pl.when(s == 0)
    def _():
        for j in range(1, shards):
            extra(j).start()

    locals_ = [
        pltpu.make_async_copy(source.at[c, s], held.at[s, c], own_sem.at[0]),
        pltpu.make_async_copy(hsrc.at[s], hheld.at[s], own_sem.at[1]),
    ]
    for copy in locals_:
        copy.start()

    @pl.when(s == 0)
    def _():
        copy = pltpu.make_async_copy(hspec.at[0], special, own_sem.at[2])
        copy.start()
        copy.wait()
        for j in range(1, shards):
            extra(j).wait_send()

    @pl.when(s != 0)
    def _():
        extra(s).wait_recv()

    for copy in locals_:
        copy.wait()
    for j, d in peers:
        tokens(j, d, True).wait_recv()
    for j in range(1, shards):
        spectrum(j, True).wait_recv()
    for j, d in peers:
        tokens(j, d, False).wait_send()
    for j in range(1, shards):
        spectrum(j, False).wait_send()


def scatter(source, hsrc, hspec):
    groups, shards = source.shape[:2]
    dma = pltpu.SemaphoreType.DMA
    return pl.pallas_call(
        scatter_kernel,
        out_shape=(
            jax.ShapeDtypeStruct((shards, groups) + source.shape[2:], source.dtype),
            jax.ShapeDtypeStruct(hsrc.shape, hsrc.dtype),
            jax.ShapeDtypeStruct(hspec.shape[1:], hspec.dtype),
        ),
        in_specs=[WHOLE] * 3,
        out_specs=(ANY, ANY, ANY),
        scratch_shapes=[
            dma((3,)),
            dma((groups * shards,)),
            dma((groups * shards,)),
            dma((shards,)),
            dma((shards,)),
            dma((shards,)),
            dma,
        ],
        compiler_params=pltpu.CompilerParams(collective_id=0, has_side_effects=True),
        name="scatter",
    )(source, hsrc, hspec)


def residues(shards, fan):
    bits = shards.bit_length() - 1
    flat = [2 * mirrored(r, bits) + e for r in range(shards) for e in range(2)]
    sets = [flat[i : i + fan] for i in range(0, len(flat), fan)]
    return sets + [[2 * shards] + [None] * (fan - 1)]


def transform(matrix, high, low):
    def dot(a, b):
        return jnp.dot(a, b, preferred_element_type=jnp.float32)

    return dot(matrix[0], high) + dot(matrix[0], low) + dot(matrix[1], high)


def spectral_kernel(
    fan, held, hheld, special, matrix, twiddle, result, grads, y_high, y_low, v_work, flipped
):
    shards, groups, _, rows, _ = held.shape
    bits = shards.bit_length() - 1
    length = matrix.shape[1] // 2
    sets = residues(shards, fan)
    width = LANES // fan
    pack = fan // 4
    main = len(sets) - 1
    total = 4 * shards * length
    spread = rows * fan
    near = groups // 2
    step = min(rows, 16)
    chunks = rows // step

    def zero():
        return jnp.zeros((step, LANES), jnp.float32)

    def forward(k, carry):
        c1, piece = k // chunks, k % chunks
        here = pl.ds(pl.multiple_of(piece * step, step), step)
        for sig in range(2):
            values = []
            for b in range(2 * shards):
                block = held.at[b // 2, (b % 2) * near + c1]
                left = block[0 if sig == 0 else 3, here].astype(jnp.float32)
                right = block[1 if sig == 0 else 2, here].astype(jnp.float32)
                values.append(left * right)
            found = forward_ladder(values)
            for n, slots in enumerate(sets):
                sides = []
                for p in range(2):
                    arrays = [None if f is None else found[f][p] for f in slots]
                    sides.append(
                        swap_lanes([zero() if a is None else a for a in arrays], width)
                    )
                for g in range(fan):
                    at = pl.multiple_of(c1 * spread + g * rows + piece * step, step)
                    spot = pl.ds(at, step)
                    cos, sin = twiddle[n, 0, spot, :], twiddle[n, 1, spot, :]
                    real, imag = sides[0][g], sides[1][g]
                    high, low = halves(real * cos + imag * sin)
                    lanes = slice(sig * LANES, (sig + 1) * LANES)
                    y_high[n, spot, lanes] = high
                    y_low[n, spot, lanes] = low
                    high, low = halves(imag * cos - real * sin)
                    spot = pl.ds(pl.multiple_of(length + at, step), step)
                    y_high[n, spot, lanes] = high
                    y_low[n, spot, lanes] = low
        return carry

    lax.fori_loop(0, near * chunks, forward, 0)

    flip = (
        lax.broadcasted_iota(jnp.int32, (length, length), 0)
        + lax.broadcasted_iota(jnp.int32, (length, length), 1)
        == length - 1
    )
    flip = jnp.where(flip, 1.0, 0.0).astype(jnp.bfloat16)
    share = length // pack
    first = lane_group(width) == 0
    even_lane = (lane_group(width) & 1) == 0
    extra = None

    def packets(real, imag):
        arrays = []
        for q in range(pack):
            arrays += [real[q * share : (q + 1) * share], imag[q * share : (q + 1) * share]]
        return swap_lanes(arrays, 2 * width)

    for n in range(main + 1):
        spectra = transform(matrix, y_high[n], y_low[n])
        sr, cr = spectra[:length, :LANES], spectra[:length, LANES:]
        si, ci = spectra[length:, :LANES], spectra[length:, LANES:]
        if n < main:
            devices = [n * (fan // 2) + i for i in range(fan // 2)]
            found = swap_lanes([hheld[r] for r in devices], 2 * width)
            fr = jnp.concatenate(found[0::2], axis=0)
            fi = jnp.concatenate(found[1::2], axis=0)
        else:
            small = length // 4 // 2 // pack
            pieces = [[], []]
            for q in range(pack):
                for t in range(STEPS):
                    for half in range(2):
                        block = special[t * small : (t + 1) * small]
                        for p in range(2):
                            shift = ((q * 2 + half) * 2 + p) * width
                            moved = pltpu.roll(block, LANES - shift, 1) if shift else block
                            pieces[p].append(jnp.where(first, moved, 0.0))
            fr, fi = (jnp.concatenate(piece, axis=0) for piece in pieces)
        slope_real = (sr * cr + si * ci) * (1.0 / total)
        slope_imag = (sr * ci - si * cr) * (1.0 / total)
        if n < main:
            for r, part in zip(devices, packets(slope_real, slope_imag)):
                grads[r, pl.ds(0, share, stride=2), :] = part
            slopes = jnp.concatenate([slope_real, slope_imag], axis=1)
            high, low = halves(slopes)
            turned_over = jnp.dot(flip, high, preferred_element_type=jnp.float32) + jnp.dot(
                flip, low, preferred_element_type=jnp.float32
            )
            for r, part in zip(devices, packets(turned_over[:, :LANES], -turned_over[:, LANES:])):
                flipped[r] = part
        else:
            extra = jnp.zeros((share, LANES), jnp.float32)
            for q in range(pack):
                for p, slope in enumerate((slope_real, slope_imag)):
                    place = (q * 2 + p) * 2
                    moved = slope[q * share : (q + 1) * share]
                    moved = pltpu.roll(moved, place * width, 1) if place else moved
                    extra = jnp.where(lane_group(width) == place, moved, extra)
        weight = jnp.full((1, LANES), 2.0 / total, jnp.float32)
        if None in sets[n] or 0 in sets[n]:
            weight = jnp.where(first, 1.0 / total, weight)
        conv = ((sr * fr - si * fi) * weight, (sr * fi + si * fr) * weight)
        back = ((cr * fr + ci * fi) * weight, (ci * fr - cr * fi) * weight)
        stacked = jnp.concatenate(
            [
                jnp.concatenate([conv[0], back[0]], axis=1),
                jnp.concatenate([-conv[1], -back[1]], axis=1),
            ],
            axis=0,
        )
        high, low = halves(stacked)
        found = transform(matrix, high, low)
        cos = jnp.concatenate([twiddle[n, 0]] * 2, axis=1)
        sin = jnp.concatenate([twiddle[n, 1]] * 2, axis=1)
        real, against = found[:length], found[length:]
        v_work[n, 0] = real * cos + against * sin
        v_work[n, 1] = real * sin - against * cos

    for r in range(shards):
        place = mirrored(r, bits)
        near_even = flipped[mirrored(shards - place, bits)] if place else extra
        near_odd = flipped[shards - 1 - r]
        grads[r, pl.ds(1, share, stride=2), :] = jnp.where(even_lane, near_even, near_odd)

    def inverse(k, carry):
        c1, piece = k // chunks, k % chunks
        here = pl.ds(pl.multiple_of(piece * step, step), step)
        for sig in range(2):
            values = [[None, None] for _ in range(2 * shards + 1)]
            for n, slots in enumerate(sets):
                for p in range(2):
                    arrays = []
                    for g in range(fan):
                        at = pl.multiple_of(c1 * spread + g * rows + piece * step, step)
                        lanes = slice(sig * LANES, (sig + 1) * LANES)
                        arrays.append(v_work[n, p, pl.ds(at, step), lanes])
                    for f, array in zip(slots, swap_lanes(arrays, width)):
                        if f is not None:
                            values[f][p] = array
            for b, value in enumerate(inverse_ladder([tuple(v) for v in values])):
                result[b // 2, (b % 2) * near + c1, sig, here, :] = value
        return carry

    lax.fori_loop(0, near * chunks, inverse, 0)


def spectral(held, hheld, special, tables, fan):
    shards, groups, _, rows, _ = held.shape
    matrix, twiddle = tables
    sets, _, length, _ = twiddle.shape
    return pl.pallas_call(
        functools.partial(spectral_kernel, fan),
        out_shape=(
            jax.ShapeDtypeStruct((shards, groups, 2, rows, LANES), jnp.float32),
            jax.ShapeDtypeStruct((shards, 2 * hheld.shape[1], LANES), jnp.float32),
        ),
        in_specs=[WHOLE] * 5,
        out_specs=(WHOLE, WHOLE),
        scratch_shapes=[
            pltpu.VMEM((sets, 2 * length, 2 * LANES), jnp.bfloat16),
            pltpu.VMEM((sets, 2 * length, 2 * LANES), jnp.bfloat16),
            pltpu.VMEM((sets, 2, length, 2 * LANES), jnp.float32),
            pltpu.VMEM(hheld.shape, jnp.float32),
        ],
        compiler_params=pltpu.CompilerParams(vmem_limit_bytes=48 * 1024 * 1024),
        name="spectral",
    )(held, hheld, special, matrix, twiddle)


def deliver_kernel(source, grads, target, landed, own_sem, t_send, t_recv, g_send, g_recv):
    shards, groups = source.shape[:2]
    s, c = lax.axis_index("seq"), lax.axis_index("chan")
    peers = [(j, d) for d in range(groups - 1, -1, -1) for j in range(shards) if j or d]
    meet([(s ^ j, c ^ d) for j, d in peers])

    def tokens(j, d, landing):
        to_s, to_c = (s ^ j, c ^ d) if landing else (s, c)
        return pltpu.make_async_remote_copy(
            src_ref=source.at[s ^ j, c ^ d],
            dst_ref=target.at[to_c, to_s],
            send_sem=t_send.at[d * shards + j],
            recv_sem=t_recv.at[d * shards + j],
            device_id=(s ^ j, c ^ d),
            device_id_type=MESH,
        )

    def slopes(j, landing):
        return pltpu.make_async_remote_copy(
            src_ref=grads.at[s ^ j],
            dst_ref=landed.at[s ^ j] if landing else landed.at[s],
            send_sem=g_send.at[j],
            recv_sem=g_recv.at[j],
            device_id=(s ^ j, c),
            device_id_type=MESH,
        )

    for j in range(1, shards):
        slopes(j, False).start()
    for j, d in peers:
        tokens(j, d, False).start()
    locals_ = [
        pltpu.make_async_copy(source.at[s, c], target.at[c, s], own_sem.at[0]),
        pltpu.make_async_copy(grads.at[s], landed.at[s], own_sem.at[1]),
    ]
    for copy in locals_:
        copy.start()
    for copy in locals_:
        copy.wait()
    for j, d in peers:
        tokens(j, d, True).wait_recv()
    for j in range(1, shards):
        slopes(j, True).wait_recv()
    for j, d in peers:
        tokens(j, d, False).wait_send()
    for j in range(1, shards):
        slopes(j, False).wait_send()


def deliver(source, grads):
    shards, groups = source.shape[:2]
    dma = pltpu.SemaphoreType.DMA
    return pl.pallas_call(
        deliver_kernel,
        out_shape=(
            jax.ShapeDtypeStruct((groups, shards) + source.shape[2:], source.dtype),
            jax.ShapeDtypeStruct(grads.shape, grads.dtype),
        ),
        in_specs=[WHOLE] * 2,
        out_specs=(ANY, ANY),
        scratch_shapes=[
            dma((2,)),
            dma((groups * shards,)),
            dma((groups * shards,)),
            dma((shards,)),
            dma((shards,)),
        ],
        compiler_params=pltpu.CompilerParams(collective_id=1, has_side_effects=True),
        name="deliver",
    )(source, grads)


def finish_kernel(width, values, gate_in, gate_out, cotangent, found, landed, *outs):
    fan, rows = found.shape[0], found.shape[2]
    conv = swap_lanes([found[u, 0] for u in range(fan)], width)
    back = swap_lanes([found[u, 1] for u in range(fan)], width)
    for g in range(fan):
        here = slice(g * rows, (g + 1) * rows)

        def wide(ref):
            return ref[here].astype(jnp.float32)

        outs[0][here] = (wide(gate_out) * conv[g]).astype(jnp.bfloat16)
        outs[1][here] = (back[g] * wide(gate_in)).astype(jnp.bfloat16)
        outs[2][here] = (back[g] * wide(values)).astype(jnp.bfloat16)
        outs[3][here] = (wide(cotangent) * conv[g]).astype(jnp.bfloat16)
    slopes = swap_lanes([landed[u] for u in range(fan)], width)
    for i, slope in enumerate(slopes):
        outs[4][i // 2 % 2, i % 2, i // 4] = slope


def finish(inputs, found, landed, filt):
    rows, channels = inputs[0].shape
    devices, _, short, _ = found.shape
    width = channels // devices
    fan = LANES // width
    pack = fan // 4
    wide = landed.shape[1]
    column = pl.BlockSpec((rows, LANES), lambda t: (0, t))
    blocks = channels // LANES
    outs = pl.pallas_call(
        functools.partial(finish_kernel, width),
        grid=(blocks,),
        out_shape=tuple(jax.ShapeDtypeStruct((rows, channels), jnp.bfloat16) for _ in range(4))
        + (jax.ShapeDtypeStruct((2, 2, pack, wide, filt.shape[4]), jnp.float32),),
        in_specs=[column] * 4
        + [
            pl.BlockSpec((fan, 2, short, LANES), lambda t: (t, 0, 0, 0)),
            pl.BlockSpec((fan, wide // STEPS, LANES), lambda t: (t // STEPS, t % STEPS, 0)),
        ],
        out_specs=(column,) * 4
        + (
            pl.BlockSpec(
                (2, 2, pack, wide // STEPS, LANES),
                lambda t: (0, 0, 0, t % STEPS, t // STEPS),
            ),
        ),
        name="finish",
    )(*inputs, found, landed)
    return outs[:4] + (outs[4].reshape(filt.shape),)


def make_tables(shards, fan, length):
    counter = np.arange(length)
    angle = 2.0 * math.pi * (np.outer(counter, counter) % length) / length
    cos, sin = np.cos(angle), np.sin(angle)
    whole = np.block([[cos, sin], [-sin, cos]])
    high = whole.astype(jnp.bfloat16)
    low = (whole - high.astype(np.float64)).astype(jnp.bfloat16)
    total = 4 * shards * length
    turns = []
    for slots in residues(shards, fan):
        lanes = np.repeat([0 if f is None else f for f in slots], LANES // fan)
        turn = 2.0 * math.pi * (counter[:, None] * lanes[None, :] % total) / total
        turns.append(np.stack([np.cos(turn), np.sin(turn)]))
    twiddle = np.stack(turns).astype(np.float32)
    return jnp.asarray(np.stack([high, low])), jnp.asarray(twiddle)


def on_device(shards, groups, values_in, gate_in, gate_out, cotangent, filter_spectra):
    inputs = (values_in, gate_in, gate_out, cotangent)
    rows, channels = values_in.shape
    devices = shards * groups
    fan = LANES * devices // channels
    source, hsrc, hspec = arrange(inputs, filter_spectra, devices, shards)
    source = source.reshape((groups, shards) + source.shape[1:])
    held, hheld, special = scatter(source, hsrc, hspec)
    tables = make_tables(shards, fan, rows * groups // 2)
    result, grads = spectral(held, hheld, special, tables, fan)
    found, landed = deliver(result, grads)
    found = found.reshape((devices,) + found.shape[2:])
    return finish(inputs, found, landed, filter_spectra)


def solution(mesh):
    tokens = P(("seq", "chan"), None)
    spectrum = P(None, "seq", None, None, "chan")
    return jax.shard_map(
        functools.partial(on_device, mesh.shape["seq"], mesh.shape["chan"]),
        mesh=mesh,
        in_specs=(tokens, tokens, tokens, tokens, spectrum),
        out_specs=(tokens, tokens, tokens, tokens, spectrum),
        check_vma=False,
    )
```

```python
import functools
import math

import jax
import jax.numpy as jnp
import numpy as np
from jax import lax
from jax.experimental import pallas as pl
from jax.experimental.pallas import tpu as pltpu
from jax.sharding import PartitionSpec as P

MESH = pl.DeviceIdType.MESH
ANY = pl.BlockSpec(memory_space=pl.ANY)
LANES = 128
STEPS = 4


def mirrored(number, bits):
    out = 0
    for place in range(bits):
        out = out + ((number >> place) & 1) * (1 << (bits - 1 - place))
    return out


def lane_group(width):
    return lax.broadcasted_iota(jnp.int32, (1, LANES), 1) // width


def swap_lanes(arrays, width):
    arrays = list(arrays)
    group = lane_group(width)
    bit = 1
    while bit < len(arrays):
        low = (group & bit) == 0
        shift = bit * width
        for i in range(len(arrays)):
            if i & bit:
                continue
            a, b = arrays[i], arrays[i | bit]
            arrays[i] = jnp.where(low, a, pltpu.roll(b, shift, 1))
            arrays[i | bit] = jnp.where(low, pltpu.roll(a, LANES - shift, 1), b)
        bit *= 2
    return arrays


def halves(data):
    high = data.astype(jnp.bfloat16)
    return high, (data - high.astype(jnp.float32)).astype(jnp.bfloat16)


def add(a, b):
    if a is None:
        return b
    return a if b is None else a + b


def sub(a, b):
    if b is None:
        return a
    return -b if a is None else a - b


def scale(a, factor):
    if a is None or abs(factor) < 1e-12:
        return None
    if abs(factor - 1.0) < 1e-12:
        return a
    return -a if abs(factor + 1.0) < 1e-12 else a * factor


def turned(value, numerator, denominator):
    angle = 2.0 * math.pi * numerator / denominator
    cos, sin = math.cos(angle), math.sin(angle)
    real, imag = value
    return (
        sub(scale(real, cos), scale(imag, sin)),
        add(scale(real, sin), scale(imag, cos)),
    )


def conjugate(value):
    return (value[0], scale(value[1], -1.0))


def forward_ladder(values):
    if len(values) == 1:
        return [(values[0], None), (values[0], None)]
    count = 2 * len(values)
    even, odd = forward_ladder(values[0::2]), forward_ladder(values[1::2])
    out = [None] * (count // 2 + 1)
    for k in range(count // 4 + 1):
        spun = turned(odd[k], -k, count)
        out[k] = (add(even[k][0], spun[0]), add(even[k][1], spun[1]))
        if k != count // 4:
            away = (sub(even[k][0], spun[0]), sub(even[k][1], spun[1]))
            out[count // 2 - k] = conjugate(away)
    return out


def inverse_ladder(values):
    if len(values) == 2:
        return [add(values[0][0], values[1][0])]
    half = len(values) - 1
    even, odd = [], []
    for k in range(half // 2):
        a, b = values[k], conjugate(values[half - k])
        even.append((add(a[0], b[0]), add(a[1], b[1])))
        odd.append(turned((sub(a[0], b[0]), sub(a[1], b[1])), k, 2 * half))
    even.append(values[half // 2])
    odd.append(turned(values[half // 2], 1, 4))
    out = [None] * half
    out[0::2], out[1::2] = inverse_ladder(even), inverse_ladder(odd)
    return out


def residues(shards, fan):
    bits = shards.bit_length() - 1
    flat = [2 * mirrored(r, bits) + e for r in range(shards) for e in range(2)]
    sets = [flat[i : i + fan] for i in range(0, len(flat), fan)]
    return sets + [[2 * shards] + [None] * (fan - 1)]


def transform(matrix, high, low):
    def dot(a, b):
        return jnp.dot(a, b, preferred_element_type=jnp.float32)

    return dot(matrix[0], high) + dot(matrix[0], low) + dot(matrix[1], high)


def convolve_kernel(shards, groups, *refs):
    inputs, filt, matrix_in, twiddle_in, found, landed = refs[:4], *refs[4:9]
    (
        tokens,
        raw,
        matrix,
        twiddle,
        source,
        hsrc,
        hspec,
        held,
        hheld,
        special,
        y_high,
        y_low,
        v_work,
        flipped,
        grads,
        result,
        in_sem,
        own_sem,
        t_send,
        t_recv,
        f_send,
        f_recv,
        x_send,
        x_recv,
        g_send,
        g_recv,
        r_send,
        r_recv,
    ) = refs[9:]
    s, c = lax.axis_index("seq"), lax.axis_index("chan")
    devices = shards * groups
    rows = source.shape[2]
    channels = tokens.shape[2]
    width = channels // devices
    fan = LANES // width
    pack = fan // 4
    blocks = channels // LANES
    near = groups // 2
    bits = shards.bit_length() - 1
    length = matrix.shape[1] // 2
    total = 4 * shards * length
    spread = rows * fan
    step = min(rows, 16)
    chunks = rows // step
    share = length // pack
    sets = residues(shards, fan)
    main = len(sets) - 1

    loads = [pltpu.make_async_copy(inputs[a], tokens.at[a], in_sem.at[a]) for a in range(4)]
    loads.append(pltpu.make_async_copy(matrix_in, matrix, in_sem.at[4]))
    loads.append(pltpu.make_async_copy(twiddle_in, twiddle, in_sem.at[5]))
    for i in range(raw.shape[0]):
        part = filt.at[:, :, :, :, pl.ds(i * LANES, LANES)]
        loads.append(pltpu.make_async_copy(part, raw.at[i], in_sem.at[6 + i]))
    for load in loads:
        load.start()

    peers = [(j, d) for d in range(groups - 1, -1, -1) for j in range(shards) if j or d]
    barrier = pltpu.get_barrier_semaphore()
    for j, d in peers:
        pl.semaphore_signal(barrier, inc=1, device_id=(s ^ j, c ^ d), device_id_type=MESH)

    def token(j, d, landing):
        to_s, to_c = (s ^ j, c ^ d) if landing else (s, c)
        return pltpu.make_async_remote_copy(
            src_ref=source.at[(c ^ d) * shards + (s ^ j)],
            dst_ref=held.at[to_s, to_c],
            send_sem=t_send.at[d * shards + j],
            recv_sem=t_recv.at[d * shards + j],
            device_id=(s ^ j, c ^ d),
            device_id_type=MESH,
        )

    def spectrum(j, landing):
        return pltpu.make_async_remote_copy(
            src_ref=hsrc.at[s ^ j],
            dst_ref=hheld.at[s ^ j] if landing else hheld.at[s],
            send_sem=f_send.at[j],
            recv_sem=f_recv.at[j],
            device_id=(s ^ j, c),
            device_id_type=MESH,
        )

    def extra(j):
        return pltpu.make_async_remote_copy(
            src_ref=hspec.at[j],
            dst_ref=special,
            send_sem=x_send.at[j],
            recv_sem=x_recv,
            device_id=(j, c),
            device_id_type=MESH,
        )

    def slope(odd, r):
        return pltpu.make_async_remote_copy(
            src_ref=grads.at[odd, r],
            dst_ref=landed.at[odd, s],
            send_sem=g_send.at[odd, r],
            recv_sem=g_recv.at[odd, s],
            device_id=(r, c),
            device_id_type=MESH,
        )

    def arrival(odd, r):
        return pltpu.make_async_remote_copy(
            src_ref=grads.at[odd, r],
            dst_ref=landed.at[odd, r],
            send_sem=g_send.at[odd, r],
            recv_sem=g_recv.at[odd, r],
            device_id=(r, c),
            device_id_type=MESH,
        )

    def outcome(j, d, landing):
        to_s, to_c = (s ^ j, c ^ d) if landing else (s, c)
        return pltpu.make_async_remote_copy(
            src_ref=result.at[s ^ j, c ^ d],
            dst_ref=found.at[to_c * shards + to_s],
            send_sem=r_send.at[d * shards + j],
            recv_sem=r_recv.at[d * shards + j],
            device_id=(s ^ j, c ^ d),
            device_id_type=MESH,
        )

    for a in range(4):
        loads[a].wait()

    def arrange(t, carry):
        lanes = pl.ds(pl.multiple_of(t * LANES, LANES), LANES)
        for a in range(4):
            parts = [
                tokens[a, g * rows : (g + 1) * rows, lanes].astype(jnp.float32)
                for g in range(fan)
            ]
            for u, part in enumerate(swap_lanes(parts, width)):
                source[t * fan + u, a] = part.astype(jnp.bfloat16)
        return carry

    lax.fori_loop(0, blocks, arrange, 0)
    pl.semaphore_wait(barrier, len(peers))
    for j, d in peers:
        token(j, d, False).start()

    for load in loads[6:]:
        load.wait()
    wide = raw.shape[4]
    span = wide // 2 // STEPS

    def arrange_filter(t, carry):
        column, piece = t // STEPS, t % STEPS
        base = pl.multiple_of(piece * 2 * span, 2 * span)
        even = [
            raw[column, p, e, q, pl.ds(base, span, stride=2), :]
            for q in range(pack)
            for p in range(2)
            for e in range(2)
        ]
        for u, part in enumerate(swap_lanes(even, width)):
            hsrc[column * fan + u, pl.ds(pl.multiple_of(piece * span, span), span)] = part
        odd = [
            raw[column, p, 0, q, pl.ds(base + 1 + half * span, span // 2, stride=2), :]
            for q in range(pack)
            for half in range(2)
            for p in range(2)
        ]
        half_span = span // 2
        for u, part in enumerate(swap_lanes(odd, width)):
            at = pl.ds(pl.multiple_of(piece * half_span, half_span), half_span)
            hspec[column * fan + u, at] = part
        return carry

    lax.fori_loop(0, raw.shape[0] * STEPS, arrange_filter, 0)
    for j in range(1, shards):
        spectrum(j, False).start()
    own = [
        pltpu.make_async_copy(source.at[c * shards + s], held.at[s, c], own_sem.at[0]),
        pltpu.make_async_copy(hsrc.at[s], hheld.at[s], own_sem.at[1]),
    ]
    for copy in own:
        copy.start()

    @pl.when(s == 0)
    def _():
        for j in range(1, shards):
            extra(j).start()
        copy = pltpu.make_async_copy(hspec.at[0], special, own_sem.at[2])
        copy.start()
        copy.wait()

    own[0].wait()
    for j, d in peers:
        token(j, d, True).wait_recv()
    loads[4].wait()
    loads[5].wait()

    def zero():
        return jnp.zeros((step, LANES), jnp.float32)

    def forward(k, carry):
        c1, piece = k // chunks, k % chunks
        here = pl.ds(pl.multiple_of(piece * step, step), step)
        for sig in range(2):
            values = []
            for b in range(2 * shards):
                block = held.at[b // 2, (b % 2) * near + c1]
                left = block[0 if sig == 0 else 3, here].astype(jnp.float32)
                right = block[1 if sig == 0 else 2, here].astype(jnp.float32)
                values.append(left * right)
            ladder = forward_ladder(values)
            for n, slots in enumerate(sets):
                sides = []
                for p in range(2):
                    arrays = [None if f is None else ladder[f][p] for f in slots]
                    sides.append(
                        swap_lanes([zero() if a is None else a for a in arrays], width)
                    )
                for g in range(fan):
                    at = pl.multiple_of(c1 * spread + g * rows + piece * step, step)
                    spot = pl.ds(at, step)
                    cos, sin = twiddle[n, 0, spot, :], twiddle[n, 1, spot, :]
                    real, imag = sides[0][g], sides[1][g]
                    high, low = halves(real * cos + imag * sin)
                    lanes = slice(sig * LANES, (sig + 1) * LANES)
                    y_high[n, spot, lanes] = high
                    y_low[n, spot, lanes] = low
                    high, low = halves(imag * cos - real * sin)
                    spot = pl.ds(pl.multiple_of(length + at, step), step)
                    y_high[n, spot, lanes] = high
                    y_low[n, spot, lanes] = low
        return carry

    lax.fori_loop(0, near * chunks, forward, 0)

    flip = (
        lax.broadcasted_iota(jnp.int32, (length, length), 0)
        + lax.broadcasted_iota(jnp.int32, (length, length), 1)
        == length - 1
    )
    flip = jnp.where(flip, 1.0, 0.0).astype(jnp.bfloat16)
    first = lane_group(width) == 0
    even_lane = (lane_group(width) & 1) == 0

    def packets(real, imag):
        arrays = []
        for q in range(pack):
            arrays += [real[q * share : (q + 1) * share], imag[q * share : (q + 1) * share]]
        return swap_lanes(arrays, 2 * width)

    def members(n):
        return [n * (fan // 2) + i for i in range(fan // 2)] if n < main else []

    def send(odd, r):
        @pl.when(s != r)
        def _():
            slope(odd, r).start()

    for n in range(main + 1):
        spectra = transform(matrix, y_high[n], y_low[n])
        v_work[n, 0], v_work[n, 1] = spectra[:length], spectra[length:]
        sr, cr = spectra[:length, :LANES], spectra[:length, LANES:]
        si, ci = spectra[length:, :LANES], spectra[length:, LANES:]
        slope_real = (sr * cr + si * ci) * (1.0 / total)
        slope_imag = (sr * ci - si * cr) * (1.0 / total)
        if n < main:
            for r, part in zip(members(n), packets(slope_real, slope_imag)):
                grads[0, r] = part
            high, low = halves(jnp.concatenate([slope_real, slope_imag], axis=1))
            turned_over = jnp.dot(flip, high, preferred_element_type=jnp.float32) + jnp.dot(
                flip, low, preferred_element_type=jnp.float32
            )
            for r, part in zip(
                members(n), packets(turned_over[:, :LANES], -turned_over[:, LANES:])
            ):
                flipped[r] = part
        else:
            last = jnp.zeros((share, LANES), jnp.float32)
            for q in range(pack):
                for p, side in enumerate((slope_real, slope_imag)):
                    place = (q * 2 + p) * 2
                    moved = side[q * share : (q + 1) * share]
                    moved = pltpu.roll(moved, place * width, 1) if place else moved
                    last = jnp.where(lane_group(width) == place, moved, last)
        if n:
            for r in members(n - 1):
                send(0, r)

    for r in range(shards):
        place = mirrored(r, bits)
        near_even = flipped[mirrored(shards - place, bits)] if place else last
        grads[1, r] = jnp.where(even_lane, near_even, flipped[shards - 1 - r])

    own[1].wait()
    for j in range(1, shards):
        spectrum(j, True).wait_recv()

    @pl.when(s != 0)
    def _():
        extra(s).wait_recv()

    for n in range(main + 1):
        if n < main:
            filters = swap_lanes([hheld[r] for r in members(n)], 2 * width)
            fr = jnp.concatenate(filters[0::2], axis=0)
            fi = jnp.concatenate(filters[1::2], axis=0)
        else:
            small = length // 4 // 2 // pack
            pieces = [[], []]
            for q in range(pack):
                for t in range(STEPS):
                    for half in range(2):
                        block = special[t * small : (t + 1) * small]
                        for p in range(2):
                            shift = ((q * 2 + half) * 2 + p) * width
                            moved = pltpu.roll(block, LANES - shift, 1) if shift else block
                            pieces[p].append(jnp.where(first, moved, 0.0))
            fr, fi = (jnp.concatenate(piece, axis=0) for piece in pieces)
        weight = jnp.full((1, LANES), 2.0 / total, jnp.float32)
        if None in sets[n] or 0 in sets[n]:
            weight = jnp.where(first, 1.0 / total, weight)
        fr, fi = fr * weight, fi * weight
        sr, cr = v_work[n, 0, :, :LANES], v_work[n, 0, :, LANES:]
        si, ci = v_work[n, 1, :, :LANES], v_work[n, 1, :, LANES:]
        stacked = jnp.concatenate(
            [
                jnp.concatenate([sr * fr - si * fi, cr * fr + ci * fi], axis=1),
                jnp.concatenate([-(sr * fi + si * fr), cr * fi - ci * fr], axis=1),
            ],
            axis=0,
        )
        high, low = halves(stacked)
        sums = transform(matrix, high, low)
        cos = jnp.concatenate([twiddle[n, 0]] * 2, axis=1)
        sin = jnp.concatenate([twiddle[n, 1]] * 2, axis=1)
        real, against = sums[:length], sums[length:]
        v_work[n, 0] = real * cos + against * sin
        v_work[n, 1] = real * sin - against * cos
        if n == 0:
            for r in range(shards):
                send(1, r)

    mine = [
        pltpu.make_async_copy(grads.at[odd, s], landed.at[odd, s], own_sem.at[3 + odd])
        for odd in range(2)
    ]
    for copy in mine:
        copy.start()

    def inverse(k, carry):
        c1, piece = k // chunks, k % chunks
        here = pl.ds(pl.multiple_of(piece * step, step), step)
        for sig in range(2):
            values = [[None, None] for _ in range(2 * shards + 1)]
            for n, slots in enumerate(sets):
                for p in range(2):
                    arrays = []
                    for g in range(fan):
                        at = pl.multiple_of(c1 * spread + g * rows + piece * step, step)
                        lanes = slice(sig * LANES, (sig + 1) * LANES)
                        arrays.append(v_work[n, p, pl.ds(at, step), lanes])
                    for f, array in zip(slots, swap_lanes(arrays, width)):
                        if f is not None:
                            values[f][p] = array
            for b, value in enumerate(inverse_ladder([tuple(v) for v in values])):
                result[b // 2, (b % 2) * near + c1, sig, here, :] = value
        return carry

    lax.fori_loop(0, near * chunks, inverse, 0)
    for j, d in peers:
        outcome(j, d, False).start()
    rest = pltpu.make_async_copy(result.at[s, c], found.at[c * shards + s], own_sem.at[5])
    rest.start()

    for j, d in peers:
        token(j, d, False).wait_send()
    for j in range(1, shards):
        spectrum(j, False).wait_send()

    @pl.when(s == 0)
    def _():
        for j in range(1, shards):
            extra(j).wait_send()

    for copy in mine + [rest]:
        copy.wait()
    for odd in range(2):
        for r in range(shards):

            @pl.when(s != r)
            def _():
                arrival(odd, r).wait_recv()
                slope(odd, r).wait_send()

    for j, d in peers:
        outcome(j, d, True).wait_recv()
    for j, d in peers:
        outcome(j, d, False).wait_send()


def convolve(inputs, filt, tables, shards, groups):
    rows, channels = inputs[0].shape
    devices = shards * groups
    width = channels // devices
    fan = LANES // width
    pack = fan // 4
    short = rows // fan
    matrix, twiddle = tables
    sets, _, length, _ = twiddle.shape
    share = length // pack
    raw = filt.reshape(2, 2, pack, 2 * share, filt.shape[4])
    dma, vmem = pltpu.SemaphoreType.DMA, pltpu.VMEM
    f32, bf16 = jnp.float32, jnp.bfloat16
    return pl.pallas_call(
        functools.partial(convolve_kernel, shards, groups),
        out_shape=(
            jax.ShapeDtypeStruct((devices, 2, short, LANES), f32),
            jax.ShapeDtypeStruct((2, shards, share, LANES), f32),
        ),
        in_specs=[ANY] * 7,
        out_specs=(ANY, ANY),
        scratch_shapes=[
            vmem((4, rows, channels), bf16),
            vmem((raw.shape[4] // LANES,) + raw.shape[:4] + (LANES,), f32),
            vmem(matrix.shape, bf16),
            vmem(twiddle.shape, f32),
            vmem((devices, 4, short, LANES), bf16),
            vmem((shards, share, LANES), f32),
            vmem((shards, share // 2, LANES), f32),
            vmem((shards, groups, 4, short, LANES), bf16),
            vmem((shards, share, LANES), f32),
            vmem((share // 2, LANES), f32),
            vmem((sets, 2 * length, 2 * LANES), bf16),
            vmem((sets, 2 * length, 2 * LANES), bf16),
            vmem((sets, 2, length, 2 * LANES), f32),
            vmem((shards, share, LANES), f32),
            vmem((2, shards, share, LANES), f32),
            vmem((shards, groups, 2, short, LANES), f32),
            dma((6 + raw.shape[4] // LANES,)),
            dma((6,)),
            dma((devices,)),
            dma((devices,)),
            dma((shards,)),
            dma((shards,)),
            dma((shards,)),
            dma,
            dma((2, shards)),
            dma((2, shards)),
            dma((devices,)),
            dma((devices,)),
        ],
        compiler_params=pltpu.CompilerParams(
            collective_id=0, has_side_effects=True, vmem_limit_bytes=48 * 1024 * 1024
        ),
        name="convolve",
    )(*inputs, raw, matrix, twiddle)


def finish_kernel(width, values, gate_in, gate_out, cotangent, found, landed, *outs):
    rows = found.shape[2]
    fan = landed.shape[1]
    for block in range(found.shape[0] // fan):
        parts = [found.at[block * fan + u] for u in range(fan)]
        conv = swap_lanes([part[0] for part in parts], width)
        back = swap_lanes([part[1] for part in parts], width)
        lanes = slice(block * LANES, (block + 1) * LANES)
        for g in range(fan):
            here = slice(g * rows, (g + 1) * rows)

            def wide(ref):
                return ref[here, lanes].astype(jnp.float32)

            outs[0][here, lanes] = (wide(gate_out) * conv[g]).astype(jnp.bfloat16)
            outs[1][here, lanes] = (back[g] * wide(gate_in)).astype(jnp.bfloat16)
            outs[2][here, lanes] = (back[g] * wide(values)).astype(jnp.bfloat16)
            outs[3][here, lanes] = (wide(cotangent) * conv[g]).astype(jnp.bfloat16)
    span = landed.shape[2]
    for odd in range(2):
        for i, slope in enumerate(swap_lanes([landed[odd, u] for u in range(fan)], width)):
            outs[4][i // 2 % 2, i % 2, i // 4, pl.ds(odd, span, stride=2), :] = slope


def finish(inputs, found, landed, filt):
    rows, channels = inputs[0].shape
    devices, _, short, _ = found.shape
    width = channels // devices
    fan = LANES // width
    pack = fan // 4
    share = landed.shape[2]
    tiles = channels // LANES // STEPS
    column = pl.BlockSpec((rows, tiles * LANES), lambda t: (0, t))
    pieces = STEPS * LANES // filt.shape[4]
    outs = pl.pallas_call(
        functools.partial(finish_kernel, width),
        grid=(STEPS,),
        out_shape=tuple(jax.ShapeDtypeStruct((rows, channels), jnp.bfloat16) for _ in range(4))
        + (jax.ShapeDtypeStruct((2, 2, pack, 2 * share, filt.shape[4]), jnp.float32),),
        in_specs=[column] * 4
        + [
            pl.BlockSpec((tiles * fan, 2, short, LANES), lambda t: (t, 0, 0, 0)),
            pl.BlockSpec(
                (2, fan, share // pieces, LANES), lambda t: (0, t // pieces, t % pieces, 0)
            ),
        ],
        out_specs=(column,) * 4
        + (
            pl.BlockSpec(
                (2, 2, pack, 2 * share // pieces, LANES),
                lambda t: (0, 0, 0, t % pieces, t // pieces),
            ),
        ),
        name="finish",
    )(*inputs, found, landed)
    return outs[:4] + (outs[4].reshape(filt.shape),)


def make_tables(shards, fan, length):
    counter = np.arange(length)
    angle = 2.0 * math.pi * (np.outer(counter, counter) % length) / length
    cos, sin = np.cos(angle), np.sin(angle)
    whole = np.block([[cos, sin], [-sin, cos]])
    high = whole.astype(jnp.bfloat16)
    low = (whole - high.astype(np.float64)).astype(jnp.bfloat16)
    total = 4 * shards * length
    turns = []
    for slots in residues(shards, fan):
        lanes = np.repeat([0 if f is None else f for f in slots], LANES // fan)
        turn = 2.0 * math.pi * (counter[:, None] * lanes[None, :] % total) / total
        turns.append(np.stack([np.cos(turn), np.sin(turn)]))
    twiddle = np.stack(turns).astype(np.float32)
    return jnp.asarray(np.stack([high, low])), jnp.asarray(twiddle)


def on_device(shards, groups, values_in, gate_in, gate_out, cotangent, filter_spectra):
    inputs = (values_in, gate_in, gate_out, cotangent)
    rows, channels = values_in.shape
    fan = LANES * shards * groups // channels
    tables = make_tables(shards, fan, rows * groups // 2)
    found, landed = convolve(inputs, filter_spectra, tables, shards, groups)
    return finish(inputs, found, landed, filter_spectra)


def solution(mesh):
    tokens = P(("seq", "chan"), None)
    spectrum = P(None, "seq", None, None, "chan")
    return jax.shard_map(
        functools.partial(on_device, mesh.shape["seq"], mesh.shape["chan"]),
        mesh=mesh,
        in_specs=(tokens, tokens, tokens, tokens, spectrum),
        out_specs=(tokens, tokens, tokens, tokens, spectrum),
        check_vma=False,
    )
```

```python
import functools
import math

import jax
import jax.numpy as jnp
import numpy as np
from jax import lax
from jax.experimental import pallas as pl
from jax.experimental.pallas import tpu as pltpu
from jax.sharding import PartitionSpec as P

MESH = pl.DeviceIdType.MESH
ANY = pl.BlockSpec(memory_space=pl.ANY)
LANES = 128
STEPS = 4


def mirrored(number, bits):
    out = 0
    for place in range(bits):
        out = out + ((number >> place) & 1) * (1 << (bits - 1 - place))
    return out


def lane_group(width):
    return lax.broadcasted_iota(jnp.int32, (1, LANES), 1) // width


def swap_lanes(arrays, width):
    arrays = list(arrays)
    group = lane_group(width)
    bit = 1
    while bit < len(arrays):
        low = (group & bit) == 0
        shift = bit * width
        for i in range(len(arrays)):
            if i & bit:
                continue
            a, b = arrays[i], arrays[i | bit]
            arrays[i] = jnp.where(low, a, pltpu.roll(b, shift, 1))
            arrays[i | bit] = jnp.where(low, pltpu.roll(a, LANES - shift, 1), b)
        bit *= 2
    return arrays


def halves(data):
    high = data.astype(jnp.bfloat16)
    return high, (data - high.astype(jnp.float32)).astype(jnp.bfloat16)


def add(a, b):
    if a is None:
        return b
    return a if b is None else a + b


def sub(a, b):
    if b is None:
        return a
    return -b if a is None else a - b


def scale(a, factor):
    if a is None or abs(factor) < 1e-12:
        return None
    if abs(factor - 1.0) < 1e-12:
        return a
    return -a if abs(factor + 1.0) < 1e-12 else a * factor


def turned(value, numerator, denominator):
    angle = 2.0 * math.pi * numerator / denominator
    cos, sin = math.cos(angle), math.sin(angle)
    real, imag = value
    return (
        sub(scale(real, cos), scale(imag, sin)),
        add(scale(real, sin), scale(imag, cos)),
    )


def conjugate(value):
    return (value[0], scale(value[1], -1.0))


def forward_ladder(values):
    if len(values) == 1:
        return [(values[0], None), (values[0], None)]
    count = 2 * len(values)
    even, odd = forward_ladder(values[0::2]), forward_ladder(values[1::2])
    out = [None] * (count // 2 + 1)
    for k in range(count // 4 + 1):
        spun = turned(odd[k], -k, count)
        out[k] = (add(even[k][0], spun[0]), add(even[k][1], spun[1]))
        if k != count // 4:
            away = (sub(even[k][0], spun[0]), sub(even[k][1], spun[1]))
            out[count // 2 - k] = conjugate(away)
    return out


def inverse_ladder(values):
    if len(values) == 2:
        return [add(values[0][0], values[1][0])]
    half = len(values) - 1
    even, odd = [], []
    for k in range(half // 2):
        a, b = values[k], conjugate(values[half - k])
        even.append((add(a[0], b[0]), add(a[1], b[1])))
        odd.append(turned((sub(a[0], b[0]), sub(a[1], b[1])), k, 2 * half))
    even.append(values[half // 2])
    odd.append(turned(values[half // 2], 1, 4))
    out = [None] * half
    out[0::2], out[1::2] = inverse_ladder(even), inverse_ladder(odd)
    return out


def residues(shards, fan):
    bits = shards.bit_length() - 1
    flat = [2 * mirrored(r, bits) + e for r in range(shards) for e in range(2)]
    sets = [flat[i : i + fan] for i in range(0, len(flat), fan)]
    return sets + [[2 * shards] + [None] * (fan - 1)]


def transform(matrix, high, low):
    def dot(a, b):
        return jnp.dot(a, b, preferred_element_type=jnp.float32)

    return dot(matrix[0], high) + dot(matrix[0], low) + dot(matrix[1], high)


def convolve_kernel(shards, groups, *refs):
    inputs, filt, matrix_in, twiddle_in, found, landed = refs[:4], *refs[4:9]
    (
        tokens,
        raw,
        matrix,
        twiddle,
        source,
        hsrc,
        hspec,
        held,
        hheld,
        special,
        y_high,
        y_low,
        spectra,
        filters,
        sums,
        flipped,
        grads,
        result,
        in_sem,
        own_sem,
        t_send,
        t_recv,
        f_send,
        f_recv,
        x_send,
        x_recv,
        g_send,
        g_recv,
        r_send,
        r_recv,
    ) = refs[9:]
    s, c = lax.axis_index("seq"), lax.axis_index("chan")
    devices = shards * groups
    rows = source.shape[3]
    channels = tokens.shape[2]
    width = channels // devices
    fan = LANES // width
    pack = fan // 4
    blocks = channels // LANES
    near = groups // 2
    bits = shards.bit_length() - 1
    length = matrix.shape[1] // 2
    total = 4 * shards * length
    spread = rows * fan
    step = min(rows, 16)
    chunks = rows // step
    share = length // pack
    sets = residues(shards, fan)
    main = len(sets) - 1
    couples = [list(range(n, min(n + 2, main + 1))) for n in range(0, main + 1, 2)]

    loads = [pltpu.make_async_copy(inputs[a], tokens.at[a], in_sem.at[a]) for a in range(4)]
    loads.append(pltpu.make_async_copy(matrix_in, matrix, in_sem.at[4]))
    loads.append(pltpu.make_async_copy(twiddle_in, twiddle, in_sem.at[5]))
    for i in range(raw.shape[0]):
        part = filt.at[:, :, :, :, pl.ds(i * LANES, LANES)]
        loads.append(pltpu.make_async_copy(part, raw.at[i], in_sem.at[6 + i]))
    for load in loads:
        load.start()

    peers = [(j, d) for d in range(groups - 1, -1, -1) for j in range(shards) if j or d]
    barrier = pltpu.get_barrier_semaphore()
    for j, d in peers:
        pl.semaphore_signal(barrier, inc=1, device_id=(s ^ j, c ^ d), device_id_type=MESH)

    def token(sig, j, d, landing):
        to_s, to_c = (s ^ j, c ^ d) if landing else (s, c)
        return pltpu.make_async_remote_copy(
            src_ref=source.at[sig, (c ^ d) * shards + (s ^ j)],
            dst_ref=held.at[sig, to_s, to_c],
            send_sem=t_send.at[sig, d * shards + j],
            recv_sem=t_recv.at[sig, d * shards + j],
            device_id=(s ^ j, c ^ d),
            device_id_type=MESH,
        )

    def spectrum(j, landing):
        return pltpu.make_async_remote_copy(
            src_ref=hsrc.at[s ^ j],
            dst_ref=hheld.at[s ^ j] if landing else hheld.at[s],
            send_sem=f_send.at[j],
            recv_sem=f_recv.at[j],
            device_id=(s ^ j, c),
            device_id_type=MESH,
        )

    def extra(j):
        return pltpu.make_async_remote_copy(
            src_ref=hspec.at[j],
            dst_ref=special,
            send_sem=x_send.at[j],
            recv_sem=x_recv,
            device_id=(j, c),
            device_id_type=MESH,
        )

    def slope(odd, r):
        return pltpu.make_async_remote_copy(
            src_ref=grads.at[odd, r],
            dst_ref=landed.at[odd, s],
            send_sem=g_send.at[odd, r],
            recv_sem=g_recv.at[odd, s],
            device_id=(r, c),
            device_id_type=MESH,
        )

    def arrival(odd, r):
        return pltpu.make_async_remote_copy(
            src_ref=grads.at[odd, r],
            dst_ref=landed.at[odd, r],
            send_sem=g_send.at[odd, r],
            recv_sem=g_recv.at[odd, r],
            device_id=(r, c),
            device_id_type=MESH,
        )

    def outcome(sig, j, d, landing):
        to_s, to_c = (s ^ j, c ^ d) if landing else (s, c)
        return pltpu.make_async_remote_copy(
            src_ref=result.at[sig, s ^ j, c ^ d],
            dst_ref=found.at[sig, to_c * shards + to_s],
            send_sem=r_send.at[sig, d * shards + j],
            recv_sem=r_recv.at[sig, d * shards + j],
            device_id=(s ^ j, c ^ d),
            device_id_type=MESH,
        )

    def arrange(sig):
        for a in range(2 * sig, 2 * sig + 2):
            loads[a].wait()

        def block(t, carry):
            lanes = pl.ds(pl.multiple_of(t * LANES, LANES), LANES)
            for a in range(2):
                parts = [
                    tokens[2 * sig + a, g * rows : (g + 1) * rows, lanes].astype(jnp.float32)
                    for g in range(fan)
                ]
                for u, part in enumerate(swap_lanes(parts, width)):
                    source[sig, t * fan + u, a] = part.astype(jnp.bfloat16)
            return carry

        lax.fori_loop(0, blocks, block, 0)

    arrange(0)
    pl.semaphore_wait(barrier, len(peers))
    for j, d in peers:
        token(0, j, d, False).start()
    arrange(1)
    for load in loads[6:]:
        load.wait()
    wide = raw.shape[4]
    span = wide // 2 // STEPS

    def arrange_filter(t, carry):
        column, piece = t // STEPS, t % STEPS
        base = pl.multiple_of(piece * 2 * span, 2 * span)
        even = [
            raw[column, p, e, q, pl.ds(base, span, stride=2), :]
            for q in range(pack)
            for p in range(2)
            for e in range(2)
        ]
        for u, part in enumerate(swap_lanes(even, width)):
            hsrc[column * fan + u, pl.ds(pl.multiple_of(piece * span, span), span)] = part
        odd = [
            raw[column, p, 0, q, pl.ds(base + 1 + half * span, span // 2, stride=2), :]
            for q in range(pack)
            for half in range(2)
            for p in range(2)
        ]
        half_span = span // 2
        for u, part in enumerate(swap_lanes(odd, width)):
            at = pl.ds(pl.multiple_of(piece * half_span, half_span), half_span)
            hspec[column * fan + u, at] = part
        return carry

    lax.fori_loop(0, raw.shape[0] * STEPS, arrange_filter, 0)
    pending = list(range(1, shards))
    every = len(peers) // len(pending)
    for i, (j, d) in enumerate(peers):
        token(1, j, d, False).start()
        if pending and i % every == 0:
            spectrum(pending.pop(0), False).start()
    own = [
        pltpu.make_async_copy(
            source.at[sig, c * shards + s], held.at[sig, s, c], own_sem.at[sig]
        )
        for sig in range(2)
    ]
    own.append(pltpu.make_async_copy(hsrc.at[s], hheld.at[s], own_sem.at[2]))
    for copy in own:
        copy.start()

    @pl.when(s == 0)
    def _():
        for j in range(1, shards):
            extra(j).start()
        copy = pltpu.make_async_copy(hspec.at[0], special, own_sem.at[3])
        copy.start()
        copy.wait()

    def arrived(sig):
        own[sig].wait()
        for j, d in peers:
            token(sig, j, d, True).wait_recv()

    arrived(0)
    loads[4].wait()
    loads[5].wait()

    def zero():
        return jnp.zeros((step, LANES), jnp.float32)

    def forward(sig):
        def chunk(k, carry):
            c1, piece = k // chunks, k % chunks
            here = pl.ds(pl.multiple_of(piece * step, step), step)
            values = []
            for b in range(2 * shards):
                block = held.at[sig, b // 2, (b % 2) * near + c1]
                values.append(
                    block[0, here].astype(jnp.float32) * block[1, here].astype(jnp.float32)
                )
            ladder = forward_ladder(values)
            for n, slots in enumerate(sets):
                sides = []
                for p in range(2):
                    arrays = [None if f is None else ladder[f][p] for f in slots]
                    sides.append(
                        swap_lanes([zero() if a is None else a for a in arrays], width)
                    )
                lanes = slice(n % 2 * LANES, (n % 2 + 1) * LANES)
                for g in range(fan):
                    at = pl.multiple_of(c1 * spread + g * rows + piece * step, step)
                    spot = pl.ds(at, step)
                    cos, sin = twiddle[n, 0, spot, :], twiddle[n, 1, spot, :]
                    real, imag = sides[0][g], sides[1][g]
                    high, low = halves(real * cos + imag * sin)
                    y_high[n // 2, spot, lanes] = high
                    y_low[n // 2, spot, lanes] = low
                    high, low = halves(imag * cos - real * sin)
                    spot = pl.ds(pl.multiple_of(length + at, step), step)
                    y_high[n // 2, spot, lanes] = high
                    y_low[n // 2, spot, lanes] = low
            return carry

        lax.fori_loop(0, near * chunks, chunk, 0)

    def analyse(sig, m):
        lanes = slice(0, len(couples[m]) * LANES)
        both = transform(matrix, y_high[m, :, lanes], y_low[m, :, lanes])
        spectra[sig, m, 0, :, lanes] = both[:length]
        spectra[sig, m, 1, :, lanes] = both[length:]

    def tables(m):
        return [
            jnp.concatenate([twiddle[n, p] for n in couples[m]], axis=1) for p in range(2)
        ]

    def synthesise(sig, m):
        lanes = slice(0, len(couples[m]) * LANES)
        fr, fi = filters[m, 0, :, lanes], filters[m, 1, :, lanes]
        real, imag = spectra[sig, m, 0, :, lanes], spectra[sig, m, 1, :, lanes]
        if sig == 0:
            stacked = [real * fr - imag * fi, -(real * fi + imag * fr)]
        else:
            stacked = [real * fr + imag * fi, real * fi - imag * fr]
        high, low = halves(jnp.concatenate(stacked, axis=0))
        both = transform(matrix, high, low)
        cos, sin = tables(m)
        real, against = both[:length], both[length:]
        sums[m, 0, :, lanes] = real * cos + against * sin
        sums[m, 1, :, lanes] = real * sin - against * cos

    def inverse(sig):
        def chunk(k, carry):
            c1, piece = k // chunks, k % chunks
            here = pl.ds(pl.multiple_of(piece * step, step), step)
            values = [[None, None] for _ in range(2 * shards + 1)]
            for n, slots in enumerate(sets):
                lanes = slice(n % 2 * LANES, (n % 2 + 1) * LANES)
                for p in range(2):
                    arrays = []
                    for g in range(fan):
                        at = pl.multiple_of(c1 * spread + g * rows + piece * step, step)
                        arrays.append(sums[n // 2, p, pl.ds(at, step), lanes])
                    for f, array in zip(slots, swap_lanes(arrays, width)):
                        if f is not None:
                            values[f][p] = array
            for b, value in enumerate(inverse_ladder([tuple(v) for v in values])):
                result[sig, b // 2, (b % 2) * near + c1, here, :] = value
            return carry

        lax.fori_loop(0, near * chunks, chunk, 0)
        for j, d in peers:
            outcome(sig, j, d, False).start()

    flip = (
        lax.broadcasted_iota(jnp.int32, (length, length), 0)
        + lax.broadcasted_iota(jnp.int32, (length, length), 1)
        == length - 1
    )
    flip = jnp.where(flip, 1.0, 0.0).astype(jnp.bfloat16)
    first = lane_group(width) == 0
    even_lane = (lane_group(width) & 1) == 0

    def packets(real, imag):
        arrays = []
        for q in range(pack):
            arrays += [real[q * share : (q + 1) * share], imag[q * share : (q + 1) * share]]
        return swap_lanes(arrays, 2 * width)

    def members(n):
        return [n * (fan // 2) + i for i in range(fan // 2)] if n < main else []

    def send(odd, r):
        @pl.when(s != r)
        def _():
            slope(odd, r).start()

    forward(0)
    for m in range(len(couples)):
        analyse(0, m)

    own[2].wait()
    for j in range(1, shards):
        spectrum(j, True).wait_recv()

    @pl.when(s != 0)
    def _():
        extra(s).wait_recv()

    for n in range(main + 1):
        if n < main:
            arrays = swap_lanes([hheld[r] for r in members(n)], 2 * width)
            fr = jnp.concatenate(arrays[0::2], axis=0)
            fi = jnp.concatenate(arrays[1::2], axis=0)
        else:
            small = length // 4 // 2 // pack
            pieces = [[], []]
            for q in range(pack):
                for t in range(STEPS):
                    for half in range(2):
                        block = special[t * small : (t + 1) * small]
                        for p in range(2):
                            shift = ((q * 2 + half) * 2 + p) * width
                            moved = pltpu.roll(block, LANES - shift, 1) if shift else block
                            pieces[p].append(jnp.where(first, moved, 0.0))
            fr, fi = (jnp.concatenate(piece, axis=0) for piece in pieces)
        weight = jnp.full((1, LANES), 2.0 / total, jnp.float32)
        if None in sets[n] or 0 in sets[n]:
            weight = jnp.where(first, 1.0 / total, weight)
        lanes = slice(n % 2 * LANES, (n % 2 + 1) * LANES)
        filters[n // 2, 0, :, lanes] = fr * weight
        filters[n // 2, 1, :, lanes] = fi * weight

    for m in range(len(couples)):
        synthesise(0, m)
    inverse(0)

    arrived(1)
    forward(1)
    for n in range(main + 1):
        if n % 2 == 0:
            analyse(1, n // 2)
        lanes = slice(n % 2 * LANES, (n % 2 + 1) * LANES)
        sr, si = (spectra[0, n // 2, p, :, lanes] for p in range(2))
        cr, ci = (spectra[1, n // 2, p, :, lanes] for p in range(2))
        slope_real = (sr * cr + si * ci) * (1.0 / total)
        slope_imag = (sr * ci - si * cr) * (1.0 / total)
        if n < main:
            for r, part in zip(members(n), packets(slope_real, slope_imag)):
                grads[0, r] = part
            high, low = halves(jnp.concatenate([slope_real, slope_imag], axis=1))
            turned_over = jnp.dot(flip, high, preferred_element_type=jnp.float32) + jnp.dot(
                flip, low, preferred_element_type=jnp.float32
            )
            for r, part in zip(
                members(n), packets(turned_over[:, :LANES], -turned_over[:, LANES:])
            ):
                flipped[r] = part
        else:
            last = jnp.zeros((share, LANES), jnp.float32)
            for q in range(pack):
                for p, side in enumerate((slope_real, slope_imag)):
                    place = (q * 2 + p) * 2
                    moved = side[q * share : (q + 1) * share]
                    moved = pltpu.roll(moved, place * width, 1) if place else moved
                    last = jnp.where(lane_group(width) == place, moved, last)
        if n:
            for r in members(n - 1):
                send(0, r)

    for r in range(shards):
        place = mirrored(r, bits)
        near_even = flipped[mirrored(shards - place, bits)] if place else last
        grads[1, r] = jnp.where(even_lane, near_even, flipped[shards - 1 - r])

    for m in range(len(couples)):
        synthesise(1, m)
        if m == 0:
            for r in range(shards):
                send(1, r)
    mine = [
        pltpu.make_async_copy(grads.at[odd, s], landed.at[odd, s], own_sem.at[4 + odd])
        for odd in range(2)
    ]
    for copy in mine:
        copy.start()
    inverse(1)
    rest = pltpu.make_async_copy(
        result.at[:, s, c], found.at[:, c * shards + s], own_sem.at[6]
    )
    rest.start()

    for sig in range(2):
        for j, d in peers:
            token(sig, j, d, False).wait_send()
    for j in range(1, shards):
        spectrum(j, False).wait_send()

    @pl.when(s == 0)
    def _():
        for j in range(1, shards):
            extra(j).wait_send()

    for copy in mine + [rest]:
        copy.wait()
    for odd in range(2):
        for r in range(shards):

            @pl.when(s != r)
            def _():
                arrival(odd, r).wait_recv()
                slope(odd, r).wait_send()

    for sig in range(2):
        for j, d in peers:
            outcome(sig, j, d, True).wait_recv()
        for j, d in peers:
            outcome(sig, j, d, False).wait_send()


def convolve(inputs, filt, tables, shards, groups):
    rows, channels = inputs[0].shape
    devices = shards * groups
    width = channels // devices
    fan = LANES // width
    pack = fan // 4
    short = rows // fan
    matrix, twiddle = tables
    sets, _, length, _ = twiddle.shape
    share = length // pack
    couples = (sets + 1) // 2
    raw = filt.reshape(2, 2, pack, 2 * share, filt.shape[4])
    dma, vmem = pltpu.SemaphoreType.DMA, pltpu.VMEM
    f32, bf16 = jnp.float32, jnp.bfloat16
    return pl.pallas_call(
        functools.partial(convolve_kernel, shards, groups),
        out_shape=(
            jax.ShapeDtypeStruct((2, devices, short, LANES), f32),
            jax.ShapeDtypeStruct((2, shards, share, LANES), f32),
        ),
        in_specs=[ANY] * 7,
        out_specs=(ANY, ANY),
        scratch_shapes=[
            vmem((4, rows, channels), bf16),
            vmem((raw.shape[4] // LANES,) + raw.shape[:4] + (LANES,), f32),
            vmem(matrix.shape, bf16),
            vmem(twiddle.shape, f32),
            vmem((2, devices, 2, short, LANES), bf16),
            vmem((shards, share, LANES), f32),
            vmem((shards, share // 2, LANES), f32),
            vmem((2, shards, groups, 2, short, LANES), bf16),
            vmem((shards, share, LANES), f32),
            vmem((share // 2, LANES), f32),
            vmem((couples, 2 * length, 2 * LANES), bf16),
            vmem((couples, 2 * length, 2 * LANES), bf16),
            vmem((2, couples, 2, length, 2 * LANES), f32),
            vmem((couples, 2, length, 2 * LANES), f32),
            vmem((couples, 2, length, 2 * LANES), f32),
            vmem((shards, share, LANES), f32),
            vmem((2, shards, share, LANES), f32),
            vmem((2, shards, groups, short, LANES), f32),
            dma((6 + raw.shape[4] // LANES,)),
            dma((7,)),
            dma((2, devices)),
            dma((2, devices)),
            dma((shards,)),
            dma((shards,)),
            dma((shards,)),
            dma,
            dma((2, shards)),
            dma((2, shards)),
            dma((2, devices)),
            dma((2, devices)),
        ],
        compiler_params=pltpu.CompilerParams(
            collective_id=0, has_side_effects=True, vmem_limit_bytes=63 * 1024 * 1024
        ),
        name="convolve",
    )(*inputs, raw, matrix, twiddle)


def finish_kernel(width, values, gate_in, gate_out, cotangent, found, landed, *outs):
    rows = found.shape[2]
    fan = landed.shape[1]
    for block in range(found.shape[1] // fan):
        conv, back = (
            swap_lanes([found[sig, block * fan + u] for u in range(fan)], width)
            for sig in range(2)
        )
        lanes = slice(block * LANES, (block + 1) * LANES)
        for g in range(fan):
            here = slice(g * rows, (g + 1) * rows)

            def wide(ref):
                return ref[here, lanes].astype(jnp.float32)

            outs[0][here, lanes] = (wide(gate_out) * conv[g]).astype(jnp.bfloat16)
            outs[1][here, lanes] = (back[g] * wide(gate_in)).astype(jnp.bfloat16)
            outs[2][here, lanes] = (back[g] * wide(values)).astype(jnp.bfloat16)
            outs[3][here, lanes] = (wide(cotangent) * conv[g]).astype(jnp.bfloat16)
    span = landed.shape[2]
    for odd in range(2):
        for i, slope in enumerate(swap_lanes([landed[odd, u] for u in range(fan)], width)):
            outs[4][i // 2 % 2, i % 2, i // 4, pl.ds(odd, span, stride=2), :] = slope


def finish(inputs, found, landed, filt):
    rows, channels = inputs[0].shape
    _, devices, short, _ = found.shape
    width = channels // devices
    fan = LANES // width
    pack = fan // 4
    share = landed.shape[2]
    tiles = channels // LANES // STEPS
    column = pl.BlockSpec((rows, tiles * LANES), lambda t: (0, t))
    pieces = STEPS * LANES // filt.shape[4]
    outs = pl.pallas_call(
        functools.partial(finish_kernel, width),
        grid=(STEPS,),
        out_shape=tuple(jax.ShapeDtypeStruct((rows, channels), jnp.bfloat16) for _ in range(4))
        + (jax.ShapeDtypeStruct((2, 2, pack, 2 * share, filt.shape[4]), jnp.float32),),
        in_specs=[column] * 4
        + [
            pl.BlockSpec((2, tiles * fan, short, LANES), lambda t: (0, t, 0, 0)),
            pl.BlockSpec(
                (2, fan, share // pieces, LANES), lambda t: (0, t // pieces, t % pieces, 0)
            ),
        ],
        out_specs=(column,) * 4
        + (
            pl.BlockSpec(
                (2, 2, pack, 2 * share // pieces, LANES),
                lambda t: (0, 0, 0, t % pieces, t // pieces),
            ),
        ),
        name="finish",
    )(*inputs, found, landed)
    return outs[:4] + (outs[4].reshape(filt.shape),)


def make_tables(shards, fan, length):
    counter = np.arange(length)
    angle = 2.0 * math.pi * (np.outer(counter, counter) % length) / length
    cos, sin = np.cos(angle), np.sin(angle)
    whole = np.block([[cos, sin], [-sin, cos]])
    high = whole.astype(jnp.bfloat16)
    low = (whole - high.astype(np.float64)).astype(jnp.bfloat16)
    total = 4 * shards * length
    turns = []
    for slots in residues(shards, fan):
        lanes = np.repeat([0 if f is None else f for f in slots], LANES // fan)
        turn = 2.0 * math.pi * (counter[:, None] * lanes[None, :] % total) / total
        turns.append(np.stack([np.cos(turn), np.sin(turn)]))
    twiddle = np.stack(turns).astype(np.float32)
    return jnp.asarray(np.stack([high, low])), jnp.asarray(twiddle)


def on_device(shards, groups, values_in, gate_in, gate_out, cotangent, filter_spectra):
    inputs = (values_in, gate_in, gate_out, cotangent)
    rows, channels = values_in.shape
    fan = LANES * shards * groups // channels
    tables = make_tables(shards, fan, rows * groups // 2)
    found, landed = convolve(inputs, filter_spectra, tables, shards, groups)
    return finish(inputs, found, landed, filter_spectra)


def solution(mesh):
    tokens = P(("seq", "chan"), None)
    spectrum = P(None, "seq", None, None, "chan")
    return jax.shard_map(
        functools.partial(on_device, mesh.shape["seq"], mesh.shape["chan"]),
        mesh=mesh,
        in_specs=(tokens, tokens, tokens, tokens, spectrum),
        out_specs=(tokens, tokens, tokens, tokens, spectrum),
        check_vma=False,
    )
```

```python
import functools
import math

import jax
import jax.numpy as jnp
import numpy as np
from jax import lax
from jax.experimental import pallas as pl
from jax.experimental.pallas import tpu as pltpu
from jax.sharding import PartitionSpec as P

MESH = pl.DeviceIdType.MESH
ANY = pl.BlockSpec(memory_space=pl.ANY)
LANES = 128
STEPS = 4


def mirrored(number, bits):
    out = 0
    for place in range(bits):
        out = out + ((number >> place) & 1) * (1 << (bits - 1 - place))
    return out


def lane_group(width):
    return lax.broadcasted_iota(jnp.int32, (1, LANES), 1) // width


def swap_lanes(arrays, width):
    arrays = list(arrays)
    group = lane_group(width)
    bit = 1
    while bit < len(arrays):
        low = (group & bit) == 0
        shift = bit * width
        for i in range(len(arrays)):
            if i & bit:
                continue
            a, b = arrays[i], arrays[i | bit]
            arrays[i] = jnp.where(low, a, pltpu.roll(b, shift, 1))
            arrays[i | bit] = jnp.where(low, pltpu.roll(a, LANES - shift, 1), b)
        bit *= 2
    return arrays


def halves(data):
    high = data.astype(jnp.bfloat16)
    return high, (data - high.astype(jnp.float32)).astype(jnp.bfloat16)


def add(a, b):
    if a is None:
        return b
    return a if b is None else a + b


def sub(a, b):
    if b is None:
        return a
    return -b if a is None else a - b


def scale(a, factor):
    if a is None or abs(factor) < 1e-12:
        return None
    if abs(factor - 1.0) < 1e-12:
        return a
    return -a if abs(factor + 1.0) < 1e-12 else a * factor


def turned(value, numerator, denominator):
    angle = 2.0 * math.pi * numerator / denominator
    cos, sin = math.cos(angle), math.sin(angle)
    real, imag = value
    return (
        sub(scale(real, cos), scale(imag, sin)),
        add(scale(real, sin), scale(imag, cos)),
    )


def conjugate(value):
    return (value[0], scale(value[1], -1.0))


def forward_ladder(values):
    if len(values) == 1:
        return [(values[0], None), (values[0], None)]
    count = 2 * len(values)
    even, odd = forward_ladder(values[0::2]), forward_ladder(values[1::2])
    out = [None] * (count // 2 + 1)
    for k in range(count // 4 + 1):
        spun = turned(odd[k], -k, count)
        out[k] = (add(even[k][0], spun[0]), add(even[k][1], spun[1]))
        if k != count // 4:
            away = (sub(even[k][0], spun[0]), sub(even[k][1], spun[1]))
            out[count // 2 - k] = conjugate(away)
    return out


def inverse_ladder(values):
    if len(values) == 2:
        return [add(values[0][0], values[1][0])]
    half = len(values) - 1
    even, odd = [], []
    for k in range(half // 2):
        a, b = values[k], conjugate(values[half - k])
        even.append((add(a[0], b[0]), add(a[1], b[1])))
        odd.append(turned((sub(a[0], b[0]), sub(a[1], b[1])), k, 2 * half))
    even.append(values[half // 2])
    odd.append(turned(values[half // 2], 1, 4))
    out = [None] * half
    out[0::2], out[1::2] = inverse_ladder(even), inverse_ladder(odd)
    return out


def encode(data):
    largest = jnp.max(jnp.abs(data), axis=0, keepdims=True).astype(jnp.bfloat16)
    wide = largest.astype(jnp.float32)
    ratio = data * jnp.where(wide > 2.0**-110, 2.0**15 / jnp.maximum(wide, 2.0**-110), 0.0)
    square = ratio * ratio
    fourth = square * square
    eighth = fourth * fourth
    return jnp.where(ratio < 0.0, -eighth, eighth).astype(jnp.bfloat16), wide


def decode(code, largest):
    code = code.astype(jnp.float32)
    size = jnp.abs(code)
    root = jnp.exp2(jnp.log2(jnp.maximum(size, 2.0**-126)) * 0.125)
    root = jnp.where(size >= 2.0**-126, root, 0.0) * (largest * 2.0**-15)
    return jnp.where(code < 0.0, -root, root)


def residues(shards, fan):
    bits = shards.bit_length() - 1
    flat = [2 * mirrored(r, bits) + e for r in range(shards) for e in range(2)]
    sets = [flat[i : i + fan] for i in range(0, len(flat), fan)]
    return sets + [[2 * shards] + [None] * (fan - 1)]


def transform(matrix, high, low):
    def dot(a, b):
        return jnp.dot(a, b, preferred_element_type=jnp.float32)

    return dot(matrix[0], high) + dot(matrix[0], low) + dot(matrix[1], high)


def convolve_kernel(shards, groups, *refs):
    inputs, filt, matrix_in, twiddle_in, found, slopes = refs[:4], *refs[4:9]
    (
        tokens,
        raw,
        matrix,
        twiddle,
        source,
        hsrc,
        hspec,
        held,
        hheld,
        special,
        y_high,
        y_low,
        spectra,
        filters,
        sums,
        flipped,
        grads,
        landed,
        gathered,
        result,
        in_sem,
        own_sem,
        t_send,
        t_recv,
        f_send,
        f_recv,
        x_send,
        x_recv,
        g_send,
        g_recv,
        r_send,
        r_recv,
    ) = refs[9:]
    s, c = lax.axis_index("seq"), lax.axis_index("chan")
    devices = shards * groups
    rows = source.shape[3]
    channels = tokens.shape[2]
    width = channels // devices
    fan = LANES // width
    pack = fan // 4
    blocks = channels // LANES
    near = groups // 2
    bits = shards.bit_length() - 1
    length = matrix.shape[1] // 2
    total = 4 * shards * length
    spread = rows * fan
    step = min(rows, 16)
    chunks = rows // step
    share = length // pack
    sets = residues(shards, fan)
    main = len(sets) - 1
    couples = [list(range(n, min(n + 2, main + 1))) for n in range(0, main + 1, 2)]

    loads = [pltpu.make_async_copy(inputs[a], tokens.at[a], in_sem.at[a]) for a in range(4)]
    loads.append(pltpu.make_async_copy(matrix_in, matrix, in_sem.at[4]))
    loads.append(pltpu.make_async_copy(twiddle_in, twiddle, in_sem.at[5]))
    for i in range(raw.shape[0]):
        part = filt.at[:, :, :, :, pl.ds(i * LANES, LANES)]
        loads.append(pltpu.make_async_copy(part, raw.at[i], in_sem.at[6 + i]))
    for load in loads:
        load.start()

    peers = [(j, d) for d in range(groups) for j in range(shards) if j or d]
    barrier = pltpu.get_barrier_semaphore()
    for j, d in peers:
        pl.semaphore_signal(barrier, inc=1, device_id=(s ^ j, c ^ d), device_id_type=MESH)

    def token(sig, j, d, landing):
        to_s, to_c = (s ^ j, c ^ d) if landing else (s, c)
        return pltpu.make_async_remote_copy(
            src_ref=source.at[sig, (c ^ d) * shards + (s ^ j)],
            dst_ref=held.at[sig, to_s, to_c],
            send_sem=t_send.at[sig, d * shards + j],
            recv_sem=t_recv.at[sig, d * shards + j],
            device_id=(s ^ j, c ^ d),
            device_id_type=MESH,
        )

    def spectrum(j, landing):
        return pltpu.make_async_remote_copy(
            src_ref=hsrc.at[s ^ j],
            dst_ref=hheld.at[s ^ j] if landing else hheld.at[s],
            send_sem=f_send.at[j],
            recv_sem=f_recv.at[j],
            device_id=(s ^ j, c),
            device_id_type=MESH,
        )

    def extra(j):
        return pltpu.make_async_remote_copy(
            src_ref=hspec.at[j, pl.ds(0, share // 4)],
            dst_ref=special,
            send_sem=x_send.at[j],
            recv_sem=x_recv,
            device_id=(j, c),
            device_id_type=MESH,
        )

    def slope(odd, r):
        return pltpu.make_async_remote_copy(
            src_ref=grads.at[odd, r],
            dst_ref=landed.at[odd, s],
            send_sem=g_send.at[odd, r],
            recv_sem=g_recv.at[odd, s],
            device_id=(r, c),
            device_id_type=MESH,
        )

    def arrival(odd, r):
        return pltpu.make_async_remote_copy(
            src_ref=grads.at[odd, r],
            dst_ref=landed.at[odd, r],
            send_sem=g_send.at[odd, r],
            recv_sem=g_recv.at[odd, r],
            device_id=(r, c),
            device_id_type=MESH,
        )

    def outcome(sig, j, d, landing):
        to_s, to_c = (s ^ j, c ^ d) if landing else (s, c)
        return pltpu.make_async_remote_copy(
            src_ref=result.at[sig, s ^ j, c ^ d],
            dst_ref=found.at[sig, to_c * shards + to_s],
            send_sem=r_send.at[sig, d * shards + j],
            recv_sem=r_recv.at[sig, d * shards + j],
            device_id=(s ^ j, c ^ d),
            device_id_type=MESH,
        )

    def arrange(sig):
        for a in range(2 * sig, 2 * sig + 2):
            loads[a].wait()

        def block(t, carry):
            lanes = pl.ds(pl.multiple_of(t * LANES, LANES), LANES)
            for a in range(2):
                parts = [
                    tokens[2 * sig + a, g * rows : (g + 1) * rows, lanes].astype(jnp.float32)
                    for g in range(fan)
                ]
                for u, part in enumerate(swap_lanes(parts, width)):
                    source[sig, t * fan + u, a] = part.astype(jnp.bfloat16)
            return carry

        lax.fori_loop(0, blocks, block, 0)

    arrange(0)
    pl.semaphore_wait(barrier, len(peers))
    for j, d in peers:
        token(0, j, d, False).start()
    arrange(1)
    for load in loads[6:]:
        load.wait()
    wide = raw.shape[4]
    span = wide // 2 // STEPS

    def arrange_filter(t, carry):
        column, piece = t // STEPS, t % STEPS
        base = pl.multiple_of(piece * 2 * span, 2 * span)
        even = [
            raw[column, p, e, q, pl.ds(base, span, stride=2), :]
            for q in range(pack)
            for p in range(2)
            for e in range(2)
        ]
        for u, part in enumerate(swap_lanes(even, width)):
            hsrc[column * fan + u, pl.ds(pl.multiple_of(piece * span, span), span)] = part
        odd = [
            raw[column, p, 0, q, pl.ds(base + 1 + half * span, span // 2, stride=2), :]
            for q in range(pack)
            for half in range(2)
            for p in range(2)
        ]
        half_span = span // 2
        for u, part in enumerate(swap_lanes(odd, width)):
            at = pl.ds(pl.multiple_of(piece * half_span, half_span), half_span)
            hspec[column * fan + u, at] = part
        return carry

    lax.fori_loop(0, raw.shape[0] * STEPS, arrange_filter, 0)
    pending = list(range(1, shards))
    for j, d in peers:
        token(1, j, d, False).start()
    for j in pending:
        spectrum(j, False).start()
    own = [
        pltpu.make_async_copy(
            source.at[sig, c * shards + s], held.at[sig, s, c], own_sem.at[sig]
        )
        for sig in range(2)
    ]
    own.append(pltpu.make_async_copy(hsrc.at[s], hheld.at[s], own_sem.at[2]))
    for copy in own:
        copy.start()

    @pl.when(s == 0)
    def _():
        for j in range(1, shards):
            extra(j).start()
        copy = pltpu.make_async_copy(
            hspec.at[0, pl.ds(0, share // 4)], special, own_sem.at[3]
        )
        copy.start()
        copy.wait()

    def arrived(sig):
        own[sig].wait()
        for j, d in peers:
            token(sig, j, d, True).wait_recv()

    arrived(0)
    loads[4].wait()
    loads[5].wait()

    def zero():
        return jnp.zeros((step, LANES), jnp.float32)

    def forward(sig):
        def chunk(k, carry):
            c1, piece = k // chunks, k % chunks
            here = pl.ds(pl.multiple_of(piece * step, step), step)
            values = []
            for b in range(2 * shards):
                block = held.at[sig, b // 2, (b % 2) * near + c1]
                values.append(
                    block[0, here].astype(jnp.float32) * block[1, here].astype(jnp.float32)
                )
            ladder = forward_ladder(values)
            for n, slots in enumerate(sets):
                sides = []
                for p in range(2):
                    arrays = [None if f is None else ladder[f][p] for f in slots]
                    sides.append(
                        swap_lanes([zero() if a is None else a for a in arrays], width)
                    )
                lanes = slice(n % 2 * LANES, (n % 2 + 1) * LANES)
                for g in range(fan):
                    at = pl.multiple_of(c1 * spread + g * rows + piece * step, step)
                    spot = pl.ds(at, step)
                    cos, sin = twiddle[n, 0, spot, :], twiddle[n, 1, spot, :]
                    real, imag = sides[0][g], sides[1][g]
                    high, low = halves(real * cos + imag * sin)
                    y_high[n // 2, spot, lanes] = high
                    y_low[n // 2, spot, lanes] = low
                    high, low = halves(imag * cos - real * sin)
                    spot = pl.ds(pl.multiple_of(length + at, step), step)
                    y_high[n // 2, spot, lanes] = high
                    y_low[n // 2, spot, lanes] = low
            return carry

        lax.fori_loop(0, near * chunks, chunk, 0)

    def analyse(sig, m):
        lanes = slice(0, len(couples[m]) * LANES)
        both = transform(matrix, y_high[m, :, lanes], y_low[m, :, lanes])
        spectra[sig, m, 0, :, lanes] = both[:length]
        spectra[sig, m, 1, :, lanes] = both[length:]

    def tables(m):
        return [
            jnp.concatenate([twiddle[n, p] for n in couples[m]], axis=1) for p in range(2)
        ]

    def synthesise(sig, m):
        lanes = slice(0, len(couples[m]) * LANES)
        fr, fi = filters[m, 0, :, lanes], filters[m, 1, :, lanes]
        real, imag = spectra[sig, m, 0, :, lanes], spectra[sig, m, 1, :, lanes]
        if sig == 0:
            stacked = [real * fr - imag * fi, -(real * fi + imag * fr)]
        else:
            stacked = [real * fr + imag * fi, real * fi - imag * fr]
        high, low = halves(jnp.concatenate(stacked, axis=0))
        both = transform(matrix, high, low)
        cos, sin = tables(m)
        real, against = both[:length], both[length:]
        sums[m, 0, :, lanes] = real * cos + against * sin
        sums[m, 1, :, lanes] = real * sin - against * cos

    def inverse(sig):
        def chunk(k, carry):
            c1, piece = k // chunks, k % chunks
            here = pl.ds(pl.multiple_of(piece * step, step), step)
            values = [[None, None] for _ in range(2 * shards + 1)]
            for n, slots in enumerate(sets):
                lanes = slice(n % 2 * LANES, (n % 2 + 1) * LANES)
                for p in range(2):
                    arrays = []
                    for g in range(fan):
                        at = pl.multiple_of(c1 * spread + g * rows + piece * step, step)
                        arrays.append(sums[n // 2, p, pl.ds(at, step), lanes])
                    for f, array in zip(slots, swap_lanes(arrays, width)):
                        if f is not None:
                            values[f][p] = array
            for b, value in enumerate(inverse_ladder([tuple(v) for v in values])):
                result[sig, b // 2, (b % 2) * near + c1, here, :] = value
            return carry

        lax.fori_loop(0, near * chunks, chunk, 0)
        for j, d in peers:
            outcome(sig, j, d, False).start()

    flip = (
        lax.broadcasted_iota(jnp.int32, (length, length), 0)
        + lax.broadcasted_iota(jnp.int32, (length, length), 1)
        == length - 1
    )
    flip = jnp.where(flip, 1.0, 0.0).astype(jnp.bfloat16)
    first = lane_group(width) == 0
    even_lane = (lane_group(width) & 1) == 0

    def packets(real, imag):
        arrays = []
        for q in range(pack):
            arrays += [real[q * share : (q + 1) * share], imag[q * share : (q + 1) * share]]
        return swap_lanes(arrays, 2 * width)

    def members(n):
        return [n * (fan // 2) + i for i in range(fan // 2)] if n < main else []

    def post(odd, r, data):
        code, largest = encode(data)
        grads[odd, r, :share] = code
        grads[odd, r, share:] = jnp.broadcast_to(largest, (16, LANES)).astype(jnp.bfloat16)

    def send(odd, r):
        @pl.when(s != r)
        def _():
            slope(odd, r).start()

    forward(0)
    for m in range(len(couples)):
        analyse(0, m)

    own[2].wait()
    for j in range(1, shards):
        spectrum(j, True).wait_recv()

    @pl.when(s != 0)
    def _():
        extra(s).wait_recv()

    for n in range(main + 1):
        if n < main:
            arrays = swap_lanes([hheld[r] for r in members(n)], 2 * width)
            fr = jnp.concatenate(arrays[0::2], axis=0)
            fi = jnp.concatenate(arrays[1::2], axis=0)
        else:
            small = length // 4 // 2 // pack
            pieces = [[], []]
            for q in range(pack):
                for t in range(STEPS):
                    for half in range(2):
                        if t >= STEPS // 2:
                            for p in range(2):
                                pieces[p].append(jnp.zeros((small, LANES), jnp.float32))
                            continue
                        block = special[t * small : (t + 1) * small]
                        for p in range(2):
                            shift = ((q * 2 + half) * 2 + p) * width
                            moved = pltpu.roll(block, LANES - shift, 1) if shift else block
                            pieces[p].append(jnp.where(first, moved, 0.0))
            fr, fi = (jnp.concatenate(piece, axis=0) for piece in pieces)
        weight = jnp.full((1, LANES), 2.0 / total, jnp.float32)
        if 0 in sets[n]:
            weight = jnp.where(first, 1.0 / total, weight)
        lanes = slice(n % 2 * LANES, (n % 2 + 1) * LANES)
        filters[n // 2, 0, :, lanes] = fr * weight
        filters[n // 2, 1, :, lanes] = fi * weight

    for m in range(len(couples)):
        synthesise(0, m)
    inverse(0)

    arrived(1)
    forward(1)
    for n in range(main + 1):
        if n % 2 == 0:
            analyse(1, n // 2)
        lanes = slice(n % 2 * LANES, (n % 2 + 1) * LANES)
        sr, si = (spectra[0, n // 2, p, :, lanes] for p in range(2))
        cr, ci = (spectra[1, n // 2, p, :, lanes] for p in range(2))
        slope_real = (sr * cr + si * ci) * (1.0 / total)
        slope_imag = (sr * ci - si * cr) * (1.0 / total)
        if n < main:
            for r, part in zip(members(n), packets(slope_real, slope_imag)):
                post(0, r, part)
            high, low = halves(jnp.concatenate([slope_real, slope_imag], axis=1))
            turned_over = jnp.dot(flip, high, preferred_element_type=jnp.float32) + jnp.dot(
                flip, low, preferred_element_type=jnp.float32
            )
            for r, part in zip(
                members(n), packets(turned_over[:, :LANES], -turned_over[:, LANES:])
            ):
                flipped[r] = part
        else:
            last = jnp.zeros((share, LANES), jnp.float32)
            for q in range(pack):
                for p, side in enumerate((slope_real, slope_imag)):
                    place = (q * 2 + p) * 2
                    moved = side[q * share : (q + 1) * share]
                    moved = pltpu.roll(moved, place * width, 1) if place else moved
                    last = jnp.where(lane_group(width) == place, moved, last)
        if n:
            for r in members(n - 1):
                send(0, r)

    for r in range(shards):
        place = mirrored(r, bits)
        near_even = flipped[mirrored(shards - place, bits)] if place else last
        post(1, r, jnp.where(even_lane, near_even, flipped[shards - 1 - r]))

    for m in range(len(couples)):
        synthesise(1, m)
        if m == 0:
            for r in range(shards):
                send(1, r)
    mine = [
        pltpu.make_async_copy(grads.at[odd, s], landed.at[odd, s], own_sem.at[4 + odd])
        for odd in range(2)
    ]
    for copy in mine:
        copy.start()
    inverse(1)
    rest = pltpu.make_async_copy(
        result.at[:, s, c], found.at[:, c * shards + s], own_sem.at[6]
    )
    rest.start()

    for copy in mine:
        copy.wait()
    for odd in range(2):
        for r in range(shards):

            @pl.when(s != r)
            def _():
                arrival(odd, r).wait_recv()

    tall = share // STEPS

    def gather(t, carry):
        column, piece = t // STEPS, t % STEPS
        for odd in range(2):
            arrays = []
            for u in range(fan):
                block = landed.at[odd, column * fan + u]
                largest = block[share : share + 16].astype(jnp.float32)[0:1]
                at = pl.ds(pl.multiple_of(piece * tall, tall), tall)
                arrays.append(decode(block[at], largest))
            for i, slope_part in enumerate(swap_lanes(arrays, width)):
                at = pl.ds(2 * tall * piece + odd, tall, stride=2)
                gathered[column, i // 2 % 2, i % 2, i // 4, at, :] = slope_part
        return carry

    lax.fori_loop(0, gathered.shape[0] * STEPS, gather, 0)
    stores = [
        pltpu.make_async_copy(
            gathered.at[i],
            slopes.at[:, :, :, :, pl.ds(i * LANES, LANES)],
            own_sem.at[7 + i],
        )
        for i in range(gathered.shape[0])
    ]
    for store in stores:
        store.start()

    for sig in range(2):
        for j, d in peers:
            token(sig, j, d, False).wait_send()
    for j in range(1, shards):
        spectrum(j, False).wait_send()

    @pl.when(s == 0)
    def _():
        for j in range(1, shards):
            extra(j).wait_send()

    for odd in range(2):
        for r in range(shards):

            @pl.when(s != r)
            def _():
                slope(odd, r).wait_send()

    for copy in stores + [rest]:
        copy.wait()
    for sig in range(2):
        for j, d in peers:
            outcome(sig, j, d, True).wait_recv()
        for j, d in peers:
            outcome(sig, j, d, False).wait_send()


def convolve(inputs, filt, tables, shards, groups):
    rows, channels = inputs[0].shape
    devices = shards * groups
    width = channels // devices
    fan = LANES // width
    pack = fan // 4
    short = rows // fan
    matrix, twiddle = tables
    sets, _, length, _ = twiddle.shape
    share = length // pack
    couples = (sets + 1) // 2
    raw = filt.reshape(2, 2, pack, 2 * share, filt.shape[4])
    dma, vmem = pltpu.SemaphoreType.DMA, pltpu.VMEM
    f32, bf16 = jnp.float32, jnp.bfloat16
    return pl.pallas_call(
        functools.partial(convolve_kernel, shards, groups),
        out_shape=(
            jax.ShapeDtypeStruct((2, devices, short, LANES), f32),
            jax.ShapeDtypeStruct(raw.shape, f32),
        ),
        in_specs=[ANY] * 7,
        out_specs=(ANY, ANY),
        scratch_shapes=[
            vmem((4, rows, channels), bf16),
            vmem((raw.shape[4] // LANES,) + raw.shape[:4] + (LANES,), f32),
            vmem(matrix.shape, bf16),
            vmem(twiddle.shape, f32),
            vmem((2, devices, 2, short, LANES), bf16),
            vmem((shards, share, LANES), f32),
            vmem((shards, share // 2, LANES), f32),
            vmem((2, shards, groups, 2, short, LANES), bf16),
            vmem((shards, share, LANES), f32),
            vmem((share // 4, LANES), f32),
            vmem((couples, 2 * length, 2 * LANES), bf16),
            vmem((couples, 2 * length, 2 * LANES), bf16),
            vmem((2, couples, 2, length, 2 * LANES), f32),
            vmem((couples, 2, length, 2 * LANES), f32),
            vmem((couples, 2, length, 2 * LANES), f32),
            vmem((shards, share, LANES), f32),
            vmem((2, shards, share + 16, LANES), bf16),
            vmem((2, shards, share + 16, LANES), bf16),
            vmem((raw.shape[4] // LANES,) + raw.shape[:4] + (LANES,), f32),
            vmem((2, shards, groups, short, LANES), f32),
            dma((6 + raw.shape[4] // LANES,)),
            dma((7 + raw.shape[4] // LANES,)),
            dma((2, devices)),
            dma((2, devices)),
            dma((shards,)),
            dma((shards,)),
            dma((shards,)),
            dma,
            dma((2, shards)),
            dma((2, shards)),
            dma((2, devices)),
            dma((2, devices)),
        ],
        compiler_params=pltpu.CompilerParams(
            collective_id=0, has_side_effects=True, vmem_limit_bytes=63 * 1024 * 1024
        ),
        name="convolve",
    )(*inputs, raw, matrix, twiddle)


def finish_kernel(width, fan, values, gate_in, gate_out, cotangent, found, *outs):
    rows = found.shape[2]
    for block in range(found.shape[1] // fan):
        conv, back = (
            swap_lanes([found[sig, block * fan + u] for u in range(fan)], width)
            for sig in range(2)
        )
        lanes = slice(block * LANES, (block + 1) * LANES)
        for g in range(fan):
            here = slice(g * rows, (g + 1) * rows)

            def wide(ref):
                return ref[here, lanes].astype(jnp.float32)

            outs[0][here, lanes] = (wide(gate_out) * conv[g]).astype(jnp.bfloat16)
            outs[1][here, lanes] = (back[g] * wide(gate_in)).astype(jnp.bfloat16)
            outs[2][here, lanes] = (back[g] * wide(values)).astype(jnp.bfloat16)
            outs[3][here, lanes] = (wide(cotangent) * conv[g]).astype(jnp.bfloat16)


def finish(inputs, found):
    rows, channels = inputs[0].shape
    _, devices, short, _ = found.shape
    width = channels // devices
    fan = LANES // width
    tiles = channels // LANES // STEPS
    column = pl.BlockSpec((rows, tiles * LANES), lambda t: (0, t))
    return pl.pallas_call(
        functools.partial(finish_kernel, width, fan),
        grid=(STEPS,),
        out_shape=tuple(jax.ShapeDtypeStruct((rows, channels), jnp.bfloat16) for _ in range(4)),
        in_specs=[column] * 4
        + [pl.BlockSpec((2, tiles * fan, short, LANES), lambda t: (0, t, 0, 0))],
        out_specs=(column,) * 4,
        name="finish",
    )(*inputs, found)


def make_tables(shards, fan, length):
    counter = np.arange(length)
    angle = 2.0 * math.pi * (np.outer(counter, counter) % length) / length
    cos, sin = np.cos(angle), np.sin(angle)
    whole = np.block([[cos, sin], [-sin, cos]])
    high = whole.astype(jnp.bfloat16)
    low = (whole - high.astype(np.float64)).astype(jnp.bfloat16)
    total = 4 * shards * length
    turns = []
    for slots in residues(shards, fan):
        lanes = np.repeat([0 if f is None else f for f in slots], LANES // fan)
        turn = 2.0 * math.pi * (counter[:, None] * lanes[None, :] % total) / total
        turns.append(np.stack([np.cos(turn), np.sin(turn)]))
    twiddle = np.stack(turns).astype(np.float32)
    return jnp.asarray(np.stack([high, low])), jnp.asarray(twiddle)


def on_device(shards, groups, values_in, gate_in, gate_out, cotangent, filter_spectra):
    inputs = (values_in, gate_in, gate_out, cotangent)
    rows, channels = values_in.shape
    fan = LANES * shards * groups // channels
    tables = make_tables(shards, fan, rows * groups // 2)
    found, slopes = convolve(inputs, filter_spectra, tables, shards, groups)
    return tuple(finish(inputs, found)) + (slopes.reshape(filter_spectra.shape),)


def solution(mesh):
    tokens = P(("seq", "chan"), None)
    spectrum = P(None, "seq", None, None, "chan")
    return jax.shard_map(
        functools.partial(on_device, mesh.shape["seq"], mesh.shape["chan"]),
        mesh=mesh,
        in_specs=(tokens, tokens, tokens, tokens, spectrum),
        out_specs=(tokens, tokens, tokens, tokens, spectrum),
        check_vma=False,
    )
```

```python
import functools
import math

import jax
import jax.numpy as jnp
import numpy as np
from jax import lax
from jax.experimental import pallas as pl
from jax.experimental.pallas import tpu as pltpu
from jax.sharding import PartitionSpec as P

MESH = pl.DeviceIdType.MESH
ANY = pl.BlockSpec(memory_space=pl.ANY)
LANES = 128
STEPS = 4


def mirrored(number, bits):
    out = 0
    for place in range(bits):
        out = out + ((number >> place) & 1) * (1 << (bits - 1 - place))
    return out


def lane_group(width):
    return lax.broadcasted_iota(jnp.int32, (1, LANES), 1) // width


def swap_lanes(arrays, width):
    arrays = list(arrays)
    group = lane_group(width)
    bit = 1
    while bit < len(arrays):
        low = (group & bit) == 0
        shift = bit * width
        for i in range(len(arrays)):
            if i & bit:
                continue
            a, b = arrays[i], arrays[i | bit]
            arrays[i] = jnp.where(low, a, pltpu.roll(b, shift, 1))
            arrays[i | bit] = jnp.where(low, pltpu.roll(a, LANES - shift, 1), b)
        bit *= 2
    return arrays


def halves(data):
    high = data.astype(jnp.bfloat16)
    return high, (data - high.astype(jnp.float32)).astype(jnp.bfloat16)


def add(a, b):
    if a is None:
        return b
    return a if b is None else a + b


def sub(a, b):
    if b is None:
        return a
    return -b if a is None else a - b


def scale(a, factor):
    if a is None or abs(factor) < 1e-12:
        return None
    if abs(factor - 1.0) < 1e-12:
        return a
    return -a if abs(factor + 1.0) < 1e-12 else a * factor


def turned(value, numerator, denominator):
    angle = 2.0 * math.pi * numerator / denominator
    cos, sin = math.cos(angle), math.sin(angle)
    real, imag = value
    return (
        sub(scale(real, cos), scale(imag, sin)),
        add(scale(real, sin), scale(imag, cos)),
    )


def conjugate(value):
    return (value[0], scale(value[1], -1.0))


def forward_ladder(values):
    if len(values) == 1:
        return [(values[0], None), (values[0], None)]
    count = 2 * len(values)
    even, odd = forward_ladder(values[0::2]), forward_ladder(values[1::2])
    out = [None] * (count // 2 + 1)
    for k in range(count // 4 + 1):
        spun = turned(odd[k], -k, count)
        out[k] = (add(even[k][0], spun[0]), add(even[k][1], spun[1]))
        if k != count // 4:
            away = (sub(even[k][0], spun[0]), sub(even[k][1], spun[1]))
            out[count // 2 - k] = conjugate(away)
    return out


def inverse_ladder(values):
    if len(values) == 2:
        return [add(values[0][0], values[1][0])]
    half = len(values) - 1
    even, odd = [], []
    for k in range(half // 2):
        a, b = values[k], conjugate(values[half - k])
        even.append((add(a[0], b[0]), add(a[1], b[1])))
        odd.append(turned((sub(a[0], b[0]), sub(a[1], b[1])), k, 2 * half))
    even.append(values[half // 2])
    odd.append(turned(values[half // 2], 1, 4))
    out = [None] * half
    out[0::2], out[1::2] = inverse_ladder(even), inverse_ladder(odd)
    return out


def encode(data):
    largest = jnp.max(jnp.abs(data), axis=0, keepdims=True).astype(jnp.bfloat16)
    wide = largest.astype(jnp.float32)
    ratio = data * jnp.where(wide > 2.0**-110, 2.0**15 / jnp.maximum(wide, 2.0**-110), 0.0)
    square = ratio * ratio
    fourth = square * square
    eighth = fourth * fourth
    return jnp.where(ratio < 0.0, -eighth, eighth).astype(jnp.bfloat16), wide


def decode(code, largest):
    code = code.astype(jnp.float32)
    size = jnp.abs(code)
    root = jnp.exp2(jnp.log2(jnp.maximum(size, 2.0**-126)) * 0.125)
    root = jnp.where(size >= 2.0**-126, root, 0.0) * (largest * 2.0**-15)
    return jnp.where(code < 0.0, -root, root)


def residues(shards, fan):
    bits = shards.bit_length() - 1
    flat = [2 * mirrored(r, bits) + e for r in range(shards) for e in range(2)]
    sets = [flat[i : i + fan] for i in range(0, len(flat), fan)]
    return sets + [[2 * shards] + [None] * (fan - 1)]


def transform(matrix, high, low):
    def dot(a, b):
        return jnp.dot(a, b, preferred_element_type=jnp.float32)

    return dot(matrix[0], high) + dot(matrix[0], low) + dot(matrix[1], high)


def convolve_kernel(shards, groups, *refs):
    inputs, filt, matrix_in, twiddle_in, found, slopes = refs[:4], *refs[4:9]
    (
        tokens,
        raw,
        matrix,
        twiddle,
        source,
        hsrc,
        hspec,
        held,
        hheld,
        special,
        y_high,
        y_low,
        spectra,
        filters,
        sums,
        flipped,
        grads,
        landed,
        gathered,
        result,
        in_sem,
        own_sem,
        t_send,
        t_recv,
        f_send,
        f_recv,
        x_send,
        x_recv,
        g_send,
        g_recv,
        r_send,
        r_recv,
    ) = refs[9:]
    s, c = lax.axis_index("seq"), lax.axis_index("chan")
    devices = shards * groups
    rows = source.shape[3]
    channels = tokens.shape[2]
    width = channels // devices
    fan = LANES // width
    pack = fan // 4
    blocks = channels // LANES
    near = groups // 2
    bits = shards.bit_length() - 1
    length = matrix.shape[1] // 2
    total = 4 * shards * length
    spread = rows * fan
    step = min(rows, 16)
    chunks = rows // step
    share = length // pack
    sets = residues(shards, fan)
    main = len(sets) - 1
    couples = [list(range(n, min(n + 2, main + 1))) for n in range(0, main + 1, 2)]

    loads = [pltpu.make_async_copy(inputs[a], tokens.at[a], in_sem.at[a]) for a in range(4)]
    loads.append(pltpu.make_async_copy(matrix_in, matrix, in_sem.at[4]))
    loads.append(pltpu.make_async_copy(twiddle_in, twiddle, in_sem.at[5]))
    for i in range(raw.shape[0]):
        part = filt.at[:, :, :, :, pl.ds(i * LANES, LANES)]
        loads.append(pltpu.make_async_copy(part, raw.at[i], in_sem.at[6 + i]))
    for load in loads:
        load.start()

    peers = [(j, d) for d in range(groups) for j in range(shards) if j or d]
    barrier = pltpu.get_barrier_semaphore()
    for j, d in peers:
        pl.semaphore_signal(barrier, inc=1, device_id=(s ^ j, c ^ d), device_id_type=MESH)

    def token(sig, j, d, landing):
        to_s, to_c = (s ^ j, c ^ d) if landing else (s, c)
        return pltpu.make_async_remote_copy(
            src_ref=source.at[sig, (c ^ d) * shards + (s ^ j)],
            dst_ref=held.at[sig, to_s, to_c],
            send_sem=t_send.at[sig, d * shards + j],
            recv_sem=t_recv.at[sig, d * shards + j],
            device_id=(s ^ j, c ^ d),
            device_id_type=MESH,
        )

    def spectrum(j, landing):
        return pltpu.make_async_remote_copy(
            src_ref=hsrc.at[s ^ j],
            dst_ref=hheld.at[s ^ j] if landing else hheld.at[s],
            send_sem=f_send.at[j],
            recv_sem=f_recv.at[j],
            device_id=(s ^ j, c),
            device_id_type=MESH,
        )

    def extra(j):
        return pltpu.make_async_remote_copy(
            src_ref=hspec.at[j, pl.ds(0, share // 4)],
            dst_ref=special,
            send_sem=x_send.at[j],
            recv_sem=x_recv,
            device_id=(j, c),
            device_id_type=MESH,
        )

    def slope(odd, r):
        return pltpu.make_async_remote_copy(
            src_ref=grads.at[odd, r],
            dst_ref=landed.at[odd, s],
            send_sem=g_send.at[odd, r],
            recv_sem=g_recv.at[odd, s],
            device_id=(r, c),
            device_id_type=MESH,
        )

    def arrival(odd, r):
        return pltpu.make_async_remote_copy(
            src_ref=grads.at[odd, r],
            dst_ref=landed.at[odd, r],
            send_sem=g_send.at[odd, r],
            recv_sem=g_recv.at[odd, r],
            device_id=(r, c),
            device_id_type=MESH,
        )

    def outcome(sig, j, d, landing):
        to_s, to_c = (s ^ j, c ^ d) if landing else (s, c)
        return pltpu.make_async_remote_copy(
            src_ref=result.at[sig, s ^ j, c ^ d],
            dst_ref=found.at[sig, to_c * shards + to_s],
            send_sem=r_send.at[sig, d * shards + j],
            recv_sem=r_recv.at[sig, d * shards + j],
            device_id=(s ^ j, c ^ d),
            device_id_type=MESH,
        )

    def arrange(sig):
        for a in range(2 * sig, 2 * sig + 2):
            loads[a].wait()

        def block(t, carry):
            lanes = pl.ds(pl.multiple_of(t * LANES, LANES), LANES)
            for a in range(2):
                parts = [
                    tokens[2 * sig + a, g * rows : (g + 1) * rows, lanes].astype(jnp.float32)
                    for g in range(fan)
                ]
                for u, part in enumerate(swap_lanes(parts, width)):
                    source[sig, t * fan + u, a] = part.astype(jnp.bfloat16)
            return carry

        lax.fori_loop(0, blocks, block, 0)

    arrange(0)
    pl.semaphore_wait(barrier, len(peers))
    for j, d in peers:
        token(0, j, d, False).start()
    arrange(1)
    for load in loads[6:]:
        load.wait()
    wide = raw.shape[4]
    span = wide // 2 // STEPS

    def arrange_filter(t, carry):
        column, piece = t // STEPS, t % STEPS
        base = pl.multiple_of(piece * 2 * span, 2 * span)
        even = [
            raw[column, p, e, q, pl.ds(base, span, stride=2), :]
            for q in range(pack)
            for p in range(2)
            for e in range(2)
        ]
        for u, part in enumerate(swap_lanes(even, width)):
            hsrc[column * fan + u, pl.ds(pl.multiple_of(piece * span, span), span)] = part
        odd = [
            raw[column, p, 0, q, pl.ds(base + 1 + half * span, span // 2, stride=2), :]
            for q in range(pack)
            for half in range(2)
            for p in range(2)
        ]
        half_span = span // 2
        for u, part in enumerate(swap_lanes(odd, width)):
            at = pl.ds(pl.multiple_of(piece * half_span, half_span), half_span)
            hspec[column * fan + u, at] = part
        return carry

    lax.fori_loop(0, raw.shape[0] * STEPS, arrange_filter, 0)
    pending = list(range(1, shards))
    for j in pending:
        spectrum(j, False).start()
    for j, d in peers:
        if j < 2:
            token(1, j, d, False).start()
    own = [
        pltpu.make_async_copy(
            source.at[sig, c * shards + s], held.at[sig, s, c], own_sem.at[sig]
        )
        for sig in range(2)
    ]
    own.append(pltpu.make_async_copy(hsrc.at[s], hheld.at[s], own_sem.at[2]))
    for copy in own:
        copy.start()

    @pl.when(s == 0)
    def _():
        for j in range(1, shards):
            extra(j).start()
        copy = pltpu.make_async_copy(
            hspec.at[0, pl.ds(0, share // 4)], special, own_sem.at[3]
        )
        copy.start()
        copy.wait()

    def arrived(sig):
        own[sig].wait()
        for j, d in peers:
            token(sig, j, d, True).wait_recv()

    arrived(0)
    for j, d in peers:
        if j >= 2:
            token(1, j, d, False).start()
    loads[4].wait()
    loads[5].wait()

    def zero():
        return jnp.zeros((step, LANES), jnp.float32)

    def forward(sig):
        def chunk(k, carry):
            c1, piece = k // chunks, k % chunks
            here = pl.ds(pl.multiple_of(piece * step, step), step)
            values = []
            for b in range(2 * shards):
                block = held.at[sig, b // 2, (b % 2) * near + c1]
                values.append(
                    block[0, here].astype(jnp.float32) * block[1, here].astype(jnp.float32)
                )
            ladder = forward_ladder(values)
            for n, slots in enumerate(sets):
                sides = []
                for p in range(2):
                    arrays = [None if f is None else ladder[f][p] for f in slots]
                    sides.append(
                        swap_lanes([zero() if a is None else a for a in arrays], width)
                    )
                lanes = slice(n % 2 * LANES, (n % 2 + 1) * LANES)
                for g in range(fan):
                    at = pl.multiple_of(c1 * spread + g * rows + piece * step, step)
                    spot = pl.ds(at, step)
                    cos, sin = twiddle[n, 0, spot, :], twiddle[n, 1, spot, :]
                    real, imag = sides[0][g], sides[1][g]
                    high, low = halves(real * cos + imag * sin)
                    y_high[n // 2, spot, lanes] = high
                    y_low[n // 2, spot, lanes] = low
                    high, low = halves(imag * cos - real * sin)
                    spot = pl.ds(pl.multiple_of(length + at, step), step)
                    y_high[n // 2, spot, lanes] = high
                    y_low[n // 2, spot, lanes] = low
            return carry

        lax.fori_loop(0, near * chunks, chunk, 0)

    def analyse(sig, m):
        lanes = slice(0, len(couples[m]) * LANES)
        both = transform(matrix, y_high[m, :, lanes], y_low[m, :, lanes])
        spectra[sig, m, 0, :, lanes] = both[:length]
        spectra[sig, m, 1, :, lanes] = both[length:]

    def tables(m):
        return [
            jnp.concatenate([twiddle[n, p] for n in couples[m]], axis=1) for p in range(2)
        ]

    def synthesise(sig, m):
        lanes = slice(0, len(couples[m]) * LANES)
        fr, fi = filters[m, 0, :, lanes], filters[m, 1, :, lanes]
        real, imag = spectra[sig, m, 0, :, lanes], spectra[sig, m, 1, :, lanes]
        if sig == 0:
            stacked = [real * fr - imag * fi, -(real * fi + imag * fr)]
        else:
            stacked = [real * fr + imag * fi, real * fi - imag * fr]
        high, low = halves(jnp.concatenate(stacked, axis=0))
        both = transform(matrix, high, low)
        cos, sin = tables(m)
        real, against = both[:length], both[length:]
        sums[m, 0, :, lanes] = real * cos + against * sin
        sums[m, 1, :, lanes] = real * sin - against * cos

    def inverse(sig):
        def chunk(k, carry):
            c1, piece = k // chunks, k % chunks
            here = pl.ds(pl.multiple_of(piece * step, step), step)
            values = [[None, None] for _ in range(2 * shards + 1)]
            for n, slots in enumerate(sets):
                lanes = slice(n % 2 * LANES, (n % 2 + 1) * LANES)
                for p in range(2):
                    arrays = []
                    for g in range(fan):
                        at = pl.multiple_of(c1 * spread + g * rows + piece * step, step)
                        arrays.append(sums[n // 2, p, pl.ds(at, step), lanes])
                    for f, array in zip(slots, swap_lanes(arrays, width)):
                        if f is not None:
                            values[f][p] = array
            for b, value in enumerate(inverse_ladder([tuple(v) for v in values])):
                result[sig, b // 2, (b % 2) * near + c1, here, :] = value
            return carry

        lax.fori_loop(0, near * chunks, chunk, 0)
        for j, d in peers:
            outcome(sig, j, d, False).start()

    flip = (
        lax.broadcasted_iota(jnp.int32, (length, length), 0)
        + lax.broadcasted_iota(jnp.int32, (length, length), 1)
        == length - 1
    )
    flip = jnp.where(flip, 1.0, 0.0).astype(jnp.bfloat16)
    first = lane_group(width) == 0
    even_lane = (lane_group(width) & 1) == 0

    def packets(real, imag):
        arrays = []
        for q in range(pack):
            arrays += [real[q * share : (q + 1) * share], imag[q * share : (q + 1) * share]]
        return swap_lanes(arrays, 2 * width)

    def members(n):
        return [n * (fan // 2) + i for i in range(fan // 2)] if n < main else []

    def post(odd, r, data):
        code, largest = encode(data)
        grads[odd, r, :share] = code
        grads[odd, r, share:] = jnp.broadcast_to(largest, (16, LANES)).astype(jnp.bfloat16)

    def send(odd, r):
        @pl.when(s != r)
        def _():
            slope(odd, r).start()

    forward(0)
    for m in range(len(couples)):
        analyse(0, m)

    own[2].wait()
    for j in range(1, shards):
        spectrum(j, True).wait_recv()

    @pl.when(s != 0)
    def _():
        extra(s).wait_recv()

    for n in range(main + 1):
        if n < main:
            arrays = swap_lanes([hheld[r] for r in members(n)], 2 * width)
            fr = jnp.concatenate(arrays[0::2], axis=0)
            fi = jnp.concatenate(arrays[1::2], axis=0)
        else:
            small = length // 4 // 2 // pack
            pieces = [[], []]
            for q in range(pack):
                for t in range(STEPS):
                    for half in range(2):
                        if t >= STEPS // 2:
                            for p in range(2):
                                pieces[p].append(jnp.zeros((small, LANES), jnp.float32))
                            continue
                        block = special[t * small : (t + 1) * small]
                        for p in range(2):
                            shift = ((q * 2 + half) * 2 + p) * width
                            moved = pltpu.roll(block, LANES - shift, 1) if shift else block
                            pieces[p].append(jnp.where(first, moved, 0.0))
            fr, fi = (jnp.concatenate(piece, axis=0) for piece in pieces)
        weight = jnp.full((1, LANES), 2.0 / total, jnp.float32)
        if 0 in sets[n]:
            weight = jnp.where(first, 1.0 / total, weight)
        lanes = slice(n % 2 * LANES, (n % 2 + 1) * LANES)
        filters[n // 2, 0, :, lanes] = fr * weight
        filters[n // 2, 1, :, lanes] = fi * weight

    for m in range(len(couples)):
        synthesise(0, m)
    inverse(0)

    arrived(1)
    forward(1)
    for n in range(main + 1):
        if n % 2 == 0:
            analyse(1, n // 2)
        lanes = slice(n % 2 * LANES, (n % 2 + 1) * LANES)
        sr, si = (spectra[0, n // 2, p, :, lanes] for p in range(2))
        cr, ci = (spectra[1, n // 2, p, :, lanes] for p in range(2))
        slope_real = (sr * cr + si * ci) * (1.0 / total)
        slope_imag = (sr * ci - si * cr) * (1.0 / total)
        if n < main:
            for r, part in zip(members(n), packets(slope_real, slope_imag)):
                post(0, r, part)
            high, low = halves(jnp.concatenate([slope_real, slope_imag], axis=1))
            turned_over = jnp.dot(flip, high, preferred_element_type=jnp.float32) + jnp.dot(
                flip, low, preferred_element_type=jnp.float32
            )
            for r, part in zip(
                members(n), packets(turned_over[:, :LANES], -turned_over[:, LANES:])
            ):
                flipped[r] = part
        else:
            last = jnp.zeros((share, LANES), jnp.float32)
            for q in range(pack):
                for p, side in enumerate((slope_real, slope_imag)):
                    place = (q * 2 + p) * 2
                    moved = side[q * share : (q + 1) * share]
                    moved = pltpu.roll(moved, place * width, 1) if place else moved
                    last = jnp.where(lane_group(width) == place, moved, last)
        if n:
            for r in members(n - 1):
                send(0, r)

    for r in range(shards):
        place = mirrored(r, bits)
        near_even = flipped[mirrored(shards - place, bits)] if place else last
        post(1, r, jnp.where(even_lane, near_even, flipped[shards - 1 - r]))

    for m in range(len(couples)):
        synthesise(1, m)
        if m == 0:
            for r in range(shards):
                send(1, r)
    mine = [
        pltpu.make_async_copy(grads.at[odd, s], landed.at[odd, s], own_sem.at[4 + odd])
        for odd in range(2)
    ]
    for copy in mine:
        copy.start()
    inverse(1)
    rest = pltpu.make_async_copy(
        result.at[:, s, c], found.at[:, c * shards + s], own_sem.at[6]
    )
    rest.start()

    tall = share // STEPS

    def gather(odd):
        mine[odd].wait()
        for r in range(shards):

            @pl.when(s != r)
            def _():
                arrival(odd, r).wait_recv()

        def piece(t, carry):
            column, piece = t // STEPS, t % STEPS
            arrays = []
            for u in range(fan):
                block = landed.at[odd, column * fan + u]
                largest = block[share : share + 16].astype(jnp.float32)[0:1]
                at = pl.ds(pl.multiple_of(piece * tall, tall), tall)
                arrays.append(decode(block[at], largest))
            for i, slope_part in enumerate(swap_lanes(arrays, width)):
                at = pl.ds(2 * tall * piece + odd, tall, stride=2)
                gathered[column, i // 2 % 2, i % 2, i // 4, at, :] = slope_part
            return carry

        lax.fori_loop(0, gathered.shape[0] * STEPS, piece, 0)

    for odd in range(2):
        gather(odd)
    stores = [
        pltpu.make_async_copy(
            gathered.at[i],
            slopes.at[:, :, :, :, pl.ds(i * LANES, LANES)],
            own_sem.at[7 + i],
        )
        for i in range(gathered.shape[0])
    ]
    for store in stores:
        store.start()

    for sig in range(2):
        for j, d in peers:
            token(sig, j, d, False).wait_send()
    for j in range(1, shards):
        spectrum(j, False).wait_send()

    @pl.when(s == 0)
    def _():
        for j in range(1, shards):
            extra(j).wait_send()

    for odd in range(2):
        for r in range(shards):

            @pl.when(s != r)
            def _():
                slope(odd, r).wait_send()

    for copy in stores + [rest]:
        copy.wait()
    for sig in range(2):
        for j, d in peers:
            outcome(sig, j, d, True).wait_recv()
        for j, d in peers:
            outcome(sig, j, d, False).wait_send()


def convolve(inputs, filt, tables, shards, groups):
    rows, channels = inputs[0].shape
    devices = shards * groups
    width = channels // devices
    fan = LANES // width
    pack = fan // 4
    short = rows // fan
    matrix, twiddle = tables
    sets, _, length, _ = twiddle.shape
    share = length // pack
    couples = (sets + 1) // 2
    raw = filt.reshape(2, 2, pack, 2 * share, filt.shape[4])
    dma, vmem = pltpu.SemaphoreType.DMA, pltpu.VMEM
    f32, bf16 = jnp.float32, jnp.bfloat16
    return pl.pallas_call(
        functools.partial(convolve_kernel, shards, groups),
        out_shape=(
            jax.ShapeDtypeStruct((2, devices, short, LANES), f32),
            jax.ShapeDtypeStruct(raw.shape, f32),
        ),
        in_specs=[ANY] * 7,
        out_specs=(ANY, ANY),
        scratch_shapes=[
            vmem((4, rows, channels), bf16),
            vmem((raw.shape[4] // LANES,) + raw.shape[:4] + (LANES,), f32),
            vmem(matrix.shape, bf16),
            vmem(twiddle.shape, f32),
            vmem((2, devices, 2, short, LANES), bf16),
            vmem((shards, share, LANES), f32),
            vmem((shards, share // 2, LANES), f32),
            vmem((2, shards, groups, 2, short, LANES), bf16),
            vmem((shards, share, LANES), f32),
            vmem((share // 4, LANES), f32),
            vmem((couples, 2 * length, 2 * LANES), bf16),
            vmem((couples, 2 * length, 2 * LANES), bf16),
            vmem((2, couples, 2, length, 2 * LANES), f32),
            vmem((couples, 2, length, 2 * LANES), f32),
            vmem((couples, 2, length, 2 * LANES), f32),
            vmem((shards, share, LANES), f32),
            vmem((2, shards, share + 16, LANES), bf16),
            vmem((2, shards, share + 16, LANES), bf16),
            vmem((raw.shape[4] // LANES,) + raw.shape[:4] + (LANES,), f32),
            vmem((2, shards, groups, short, LANES), f32),
            dma((6 + raw.shape[4] // LANES,)),
            dma((7 + raw.shape[4] // LANES,)),
            dma((2, devices)),
            dma((2, devices)),
            dma((shards,)),
            dma((shards,)),
            dma((shards,)),
            dma,
            dma((2, shards)),
            dma((2, shards)),
            dma((2, devices)),
            dma((2, devices)),
        ],
        compiler_params=pltpu.CompilerParams(
            collective_id=0, has_side_effects=True, vmem_limit_bytes=63 * 1024 * 1024
        ),
        name="convolve",
    )(*inputs, raw, matrix, twiddle)


def finish_kernel(width, fan, values, gate_in, gate_out, cotangent, found, slopes, *outs):
    rows = found.shape[2]
    outs[4][...] = slopes[...]
    for block in range(found.shape[1] // fan):
        conv, back = (
            swap_lanes([found[sig, block * fan + u] for u in range(fan)], width)
            for sig in range(2)
        )
        lanes = slice(block * LANES, (block + 1) * LANES)
        for g in range(fan):
            here = slice(g * rows, (g + 1) * rows)

            def wide(ref):
                return ref[here, lanes].astype(jnp.float32)

            outs[0][here, lanes] = (wide(gate_out) * conv[g]).astype(jnp.bfloat16)
            outs[1][here, lanes] = (back[g] * wide(gate_in)).astype(jnp.bfloat16)
            outs[2][here, lanes] = (back[g] * wide(values)).astype(jnp.bfloat16)
            outs[3][here, lanes] = (wide(cotangent) * conv[g]).astype(jnp.bfloat16)


def finish(inputs, found, slopes):
    rows, channels = inputs[0].shape
    _, devices, short, _ = found.shape
    width = channels // devices
    fan = LANES // width
    steps = 2
    tiles = channels // LANES // steps
    column = pl.BlockSpec((rows, tiles * LANES), lambda t: (0, t))
    shape = slopes.shape
    part = pl.BlockSpec(shape[:3] + (shape[3] // steps, shape[4]), lambda t: (0, 0, 0, t, 0))
    return pl.pallas_call(
        functools.partial(finish_kernel, width, fan),
        grid=(steps,),
        out_shape=tuple(jax.ShapeDtypeStruct((rows, channels), jnp.bfloat16) for _ in range(4))
        + (jax.ShapeDtypeStruct(shape, jnp.float32),),
        in_specs=[column] * 4
        + [pl.BlockSpec((2, tiles * fan, short, LANES), lambda t: (0, t, 0, 0)), part],
        out_specs=(column,) * 4 + (part,),
        name="finish",
    )(*inputs, found, slopes)


def make_tables(shards, fan, length):
    counter = np.arange(length)
    angle = 2.0 * math.pi * (np.outer(counter, counter) % length) / length
    cos, sin = np.cos(angle), np.sin(angle)
    whole = np.block([[cos, sin], [-sin, cos]])
    high = whole.astype(jnp.bfloat16)
    low = (whole - high.astype(np.float64)).astype(jnp.bfloat16)
    total = 4 * shards * length
    turns = []
    for slots in residues(shards, fan):
        lanes = np.repeat([0 if f is None else f for f in slots], LANES // fan)
        turn = 2.0 * math.pi * (counter[:, None] * lanes[None, :] % total) / total
        turns.append(np.stack([np.cos(turn), np.sin(turn)]))
    twiddle = np.stack(turns).astype(np.float32)
    return jnp.asarray(np.stack([high, low])), jnp.asarray(twiddle)


def on_device(shards, groups, values_in, gate_in, gate_out, cotangent, filter_spectra):
    inputs = (values_in, gate_in, gate_out, cotangent)
    rows, channels = values_in.shape
    fan = LANES * shards * groups // channels
    tables = make_tables(shards, fan, rows * groups // 2)
    found, slopes = convolve(inputs, filter_spectra, tables, shards, groups)
    outs = finish(inputs, found, slopes)
    return tuple(outs[:4]) + (outs[4].reshape(filter_spectra.shape),)


def solution(mesh):
    tokens = P(("seq", "chan"), None)
    spectrum = P(None, "seq", None, None, "chan")
    return jax.shard_map(
        functools.partial(on_device, mesh.shape["seq"], mesh.shape["chan"]),
        mesh=mesh,
        in_specs=(tokens, tokens, tokens, tokens, spectrum),
        out_specs=(tokens, tokens, tokens, tokens, spectrum),
        check_vma=False,
    )
```

```python
import functools
import math

import jax
import jax.numpy as jnp
import numpy as np
from jax import lax
from jax.experimental import pallas as pl
from jax.experimental.pallas import tpu as pltpu
from jax.sharding import PartitionSpec as P

MESH = pl.DeviceIdType.MESH
ANY = pl.BlockSpec(memory_space=pl.ANY)
LANES = 128
STEPS = 4


def mirrored(number, bits):
    out = 0
    for place in range(bits):
        out = out + ((number >> place) & 1) * (1 << (bits - 1 - place))
    return out


def lane_group(width):
    return lax.broadcasted_iota(jnp.int32, (1, LANES), 1) // width


def swap_lanes(arrays, width):
    arrays = list(arrays)
    group = lane_group(width)
    bit = 1
    while bit < len(arrays):
        low = (group & bit) == 0
        shift = bit * width
        for i in range(len(arrays)):
            if i & bit:
                continue
            a, b = arrays[i], arrays[i | bit]
            arrays[i] = jnp.where(low, a, pltpu.roll(b, shift, 1))
            arrays[i | bit] = jnp.where(low, pltpu.roll(a, LANES - shift, 1), b)
        bit *= 2
    return arrays


def halves(data):
    high = data.astype(jnp.bfloat16)
    return high, (data - high.astype(jnp.float32)).astype(jnp.bfloat16)


def add(a, b):
    if a is None:
        return b
    return a if b is None else a + b


def sub(a, b):
    if b is None:
        return a
    return -b if a is None else a - b


def scale(a, factor):
    if a is None or abs(factor) < 1e-12:
        return None
    if abs(factor - 1.0) < 1e-12:
        return a
    return -a if abs(factor + 1.0) < 1e-12 else a * factor


def turned(value, numerator, denominator):
    angle = 2.0 * math.pi * numerator / denominator
    cos, sin = math.cos(angle), math.sin(angle)
    real, imag = value
    return (
        sub(scale(real, cos), scale(imag, sin)),
        add(scale(real, sin), scale(imag, cos)),
    )


def conjugate(value):
    return (value[0], scale(value[1], -1.0))


def forward_ladder(values):
    if len(values) == 1:
        return [(values[0], None), (values[0], None)]
    count = 2 * len(values)
    even, odd = forward_ladder(values[0::2]), forward_ladder(values[1::2])
    out = [None] * (count // 2 + 1)
    for k in range(count // 4 + 1):
        spun = turned(odd[k], -k, count)
        out[k] = (add(even[k][0], spun[0]), add(even[k][1], spun[1]))
        if k != count // 4:
            away = (sub(even[k][0], spun[0]), sub(even[k][1], spun[1]))
            out[count // 2 - k] = conjugate(away)
    return out


def inverse_ladder(values):
    if len(values) == 2:
        return [add(values[0][0], values[1][0])]
    half = len(values) - 1
    even, odd = [], []
    for k in range(half // 2):
        a, b = values[k], conjugate(values[half - k])
        even.append((add(a[0], b[0]), add(a[1], b[1])))
        odd.append(turned((sub(a[0], b[0]), sub(a[1], b[1])), k, 2 * half))
    even.append(values[half // 2])
    odd.append(turned(values[half // 2], 1, 4))
    out = [None] * half
    out[0::2], out[1::2] = inverse_ladder(even), inverse_ladder(odd)
    return out


def encode(data):
    largest = jnp.max(jnp.abs(data), axis=0, keepdims=True).astype(jnp.bfloat16)
    wide = largest.astype(jnp.float32)
    ratio = data * jnp.where(wide > 2.0**-110, 2.0**15 / jnp.maximum(wide, 2.0**-110), 0.0)
    square = ratio * ratio
    fourth = square * square
    eighth = fourth * fourth
    return jnp.where(ratio < 0.0, -eighth, eighth).astype(jnp.bfloat16), wide


def decode(code, largest):
    code = code.astype(jnp.float32)
    size = jnp.abs(code)
    root = jnp.exp2(jnp.log2(jnp.maximum(size, 2.0**-126)) * 0.125)
    root = jnp.where(size >= 2.0**-126, root, 0.0) * (largest * 2.0**-15)
    return jnp.where(code < 0.0, -root, root)


def residues(shards, fan):
    bits = shards.bit_length() - 1
    flat = [2 * mirrored(r, bits) + e for r in range(shards) for e in range(2)]
    sets = [flat[i : i + fan] for i in range(0, len(flat), fan)]
    return sets + [[2 * shards] + [None] * (fan - 1)]


def transform(matrix, high, low):
    def dot(a, b):
        return jnp.dot(a, b, preferred_element_type=jnp.float32)

    return dot(matrix[0], high) + dot(matrix[0], low) + dot(matrix[1], high)


def convolve_kernel(shards, groups, *refs):
    inputs, filt, matrix_in, twiddle_in, found, slopes = refs[:4], *refs[4:9]
    (
        tokens,
        raw,
        matrix,
        twiddle,
        source,
        hsrc,
        hspec,
        held,
        hheld,
        special,
        y_high,
        y_low,
        spectra,
        filters,
        sums,
        flipped,
        grads,
        landed,
        gathered,
        result,
        in_sem,
        own_sem,
        t_send,
        t_recv,
        f_send,
        f_recv,
        x_send,
        x_recv,
        g_send,
        g_recv,
        r_send,
        r_recv,
    ) = refs[9:]
    s, c = lax.axis_index("seq"), lax.axis_index("chan")
    devices = shards * groups
    rows = source.shape[3]
    channels = tokens.shape[2]
    width = channels // devices
    fan = LANES // width
    pack = fan // 4
    blocks = channels // LANES
    near = groups // 2
    bits = shards.bit_length() - 1
    length = matrix.shape[1] // 2
    total = 4 * shards * length
    spread = rows * fan
    step = min(rows, 16)
    chunks = rows // step
    share = length // pack
    sets = residues(shards, fan)
    main = len(sets) - 1
    couples = [list(range(n, min(n + 2, main + 1))) for n in range(0, main + 1, 2)]

    loads = [pltpu.make_async_copy(inputs[a], tokens.at[a], in_sem.at[a]) for a in range(4)]
    tables_in = [
        pltpu.make_async_copy(matrix_in, matrix, in_sem.at[4]),
        pltpu.make_async_copy(twiddle_in, twiddle, in_sem.at[5]),
    ]
    for i in range(raw.shape[0]):
        part = filt.at[:, :, :, :, pl.ds(i * LANES, LANES)]
        loads.append(pltpu.make_async_copy(part, raw.at[i], in_sem.at[6 + i]))
    for load in loads + tables_in:
        load.start()

    peers = [(j, d) for d in range(groups) for j in range(shards) if j or d]
    barrier = pltpu.get_barrier_semaphore()
    for j, d in peers:
        pl.semaphore_signal(barrier, inc=1, device_id=(s ^ j, c ^ d), device_id_type=MESH)

    def token(sig, j, d, landing):
        to_s, to_c = (s ^ j, c ^ d) if landing else (s, c)
        return pltpu.make_async_remote_copy(
            src_ref=source.at[sig, (c ^ d) * shards + (s ^ j)],
            dst_ref=held.at[sig, to_s, to_c],
            send_sem=t_send.at[sig, d * shards + j],
            recv_sem=t_recv.at[sig, d * shards + j],
            device_id=(s ^ j, c ^ d),
            device_id_type=MESH,
        )

    def spectrum(j, landing):
        return pltpu.make_async_remote_copy(
            src_ref=hsrc.at[s ^ j],
            dst_ref=hheld.at[s ^ j] if landing else hheld.at[s],
            send_sem=f_send.at[j],
            recv_sem=f_recv.at[j],
            device_id=(s ^ j, c),
            device_id_type=MESH,
        )

    def extra(j):
        return pltpu.make_async_remote_copy(
            src_ref=hspec.at[j, pl.ds(0, share // 4)],
            dst_ref=special,
            send_sem=x_send.at[j],
            recv_sem=x_recv,
            device_id=(j, c),
            device_id_type=MESH,
        )

    def slope(odd, r):
        return pltpu.make_async_remote_copy(
            src_ref=grads.at[odd, r],
            dst_ref=landed.at[odd, s],
            send_sem=g_send.at[odd, r],
            recv_sem=g_recv.at[odd, s],
            device_id=(r, c),
            device_id_type=MESH,
        )

    def arrival(odd, r):
        return pltpu.make_async_remote_copy(
            src_ref=grads.at[odd, r],
            dst_ref=landed.at[odd, r],
            send_sem=g_send.at[odd, r],
            recv_sem=g_recv.at[odd, r],
            device_id=(r, c),
            device_id_type=MESH,
        )

    def outcome(sig, j, d, landing):
        to_s, to_c = (s ^ j, c ^ d) if landing else (s, c)
        return pltpu.make_async_remote_copy(
            src_ref=result.at[sig, s ^ j, c ^ d],
            dst_ref=found.at[sig, to_c * shards + to_s],
            send_sem=r_send.at[sig, d * shards + j],
            recv_sem=r_recv.at[sig, d * shards + j],
            device_id=(s ^ j, c ^ d),
            device_id_type=MESH,
        )

    def arrange(sig):
        for a in range(2 * sig, 2 * sig + 2):
            loads[a].wait()

        def block(t, carry):
            lanes = pl.ds(pl.multiple_of(t * LANES, LANES), LANES)
            for a in range(2):
                parts = [
                    tokens[2 * sig + a, g * rows : (g + 1) * rows, lanes].astype(jnp.float32)
                    for g in range(fan)
                ]
                for u, part in enumerate(swap_lanes(parts, width)):
                    source[sig, t * fan + u, a] = part.astype(jnp.bfloat16)
            return carry

        lax.fori_loop(0, blocks, block, 0)

    arrange(0)
    pl.semaphore_wait(barrier, len(peers))
    for j, d in peers:
        token(0, j, d, False).start()
    for load in loads[4:]:
        load.wait()
    wide = raw.shape[4]
    span = wide // 2 // STEPS

    def arrange_filter(t, carry):
        column, piece = t // STEPS, t % STEPS
        base = pl.multiple_of(piece * 2 * span, 2 * span)
        even = [
            raw[column, p, e, q, pl.ds(base, span, stride=2), :]
            for q in range(pack)
            for p in range(2)
            for e in range(2)
        ]
        for u, part in enumerate(swap_lanes(even, width)):
            hsrc[column * fan + u, pl.ds(pl.multiple_of(piece * span, span), span)] = part
        odd = [
            raw[column, p, 0, q, pl.ds(base + 1 + half * span, span // 2, stride=2), :]
            for q in range(pack)
            for half in range(2)
            for p in range(2)
        ]
        half_span = span // 2
        for u, part in enumerate(swap_lanes(odd, width)):
            at = pl.ds(pl.multiple_of(piece * half_span, half_span), half_span)
            hspec[column * fan + u, at] = part
        return carry

    lax.fori_loop(0, raw.shape[0] * STEPS, arrange_filter, 0)
    pending = list(range(1, shards))
    for j in pending:
        spectrum(j, False).start()
    arrange(1)
    for j, d in peers:
        if j < 2:
            token(1, j, d, False).start()
    own = [
        pltpu.make_async_copy(
            source.at[sig, c * shards + s], held.at[sig, s, c], own_sem.at[sig]
        )
        for sig in range(2)
    ]
    own.append(pltpu.make_async_copy(hsrc.at[s], hheld.at[s], own_sem.at[2]))
    for copy in own:
        copy.start()

    @pl.when(s == 0)
    def _():
        for j in range(1, shards):
            extra(j).start()
        copy = pltpu.make_async_copy(
            hspec.at[0, pl.ds(0, share // 4)], special, own_sem.at[3]
        )
        copy.start()
        copy.wait()

    def arrived(sig):
        own[sig].wait()
        for j, d in peers:
            token(sig, j, d, True).wait_recv()

    arrived(0)
    for j, d in peers:
        if j >= 2:
            token(1, j, d, False).start()
    for load in tables_in:
        load.wait()

    def zero():
        return jnp.zeros((step, LANES), jnp.float32)

    def forward(sig):
        def chunk(k, carry):
            c1, piece = k // chunks, k % chunks
            here = pl.ds(pl.multiple_of(piece * step, step), step)
            values = []
            for b in range(2 * shards):
                block = held.at[sig, b // 2, (b % 2) * near + c1]
                values.append(
                    block[0, here].astype(jnp.float32) * block[1, here].astype(jnp.float32)
                )
            ladder = forward_ladder(values)
            for n, slots in enumerate(sets):
                sides = []
                for p in range(2):
                    arrays = [None if f is None else ladder[f][p] for f in slots]
                    sides.append(
                        swap_lanes([zero() if a is None else a for a in arrays], width)
                    )
                lanes = slice(n % 2 * LANES, (n % 2 + 1) * LANES)
                for g in range(fan):
                    at = pl.multiple_of(c1 * spread + g * rows + piece * step, step)
                    spot = pl.ds(at, step)
                    cos, sin = twiddle[n, 0, spot, :], twiddle[n, 1, spot, :]
                    real, imag = sides[0][g], sides[1][g]
                    high, low = halves(real * cos + imag * sin)
                    y_high[n // 2, spot, lanes] = high
                    y_low[n // 2, spot, lanes] = low
                    high, low = halves(imag * cos - real * sin)
                    spot = pl.ds(pl.multiple_of(length + at, step), step)
                    y_high[n // 2, spot, lanes] = high
                    y_low[n // 2, spot, lanes] = low
            return carry

        lax.fori_loop(0, near * chunks, chunk, 0)

    def analyse(sig, m):
        lanes = slice(0, len(couples[m]) * LANES)
        both = transform(matrix, y_high[m, :, lanes], y_low[m, :, lanes])
        spectra[sig, m, 0, :, lanes] = both[:length]
        spectra[sig, m, 1, :, lanes] = both[length:]

    def tables(m):
        return [
            jnp.concatenate([twiddle[n, p] for n in couples[m]], axis=1) for p in range(2)
        ]

    def synthesise(sig, m):
        lanes = slice(0, len(couples[m]) * LANES)
        fr, fi = filters[m, 0, :, lanes], filters[m, 1, :, lanes]
        real, imag = spectra[sig, m, 0, :, lanes], spectra[sig, m, 1, :, lanes]
        if sig == 0:
            stacked = [real * fr - imag * fi, -(real * fi + imag * fr)]
        else:
            stacked = [real * fr + imag * fi, real * fi - imag * fr]
        high, low = halves(jnp.concatenate(stacked, axis=0))
        both = transform(matrix, high, low)
        cos, sin = tables(m)
        real, against = both[:length], both[length:]
        sums[m, 0, :, lanes] = real * cos + against * sin
        sums[m, 1, :, lanes] = real * sin - against * cos

    def inverse(sig):
        def chunk(k, carry):
            c1, piece = k // chunks, k % chunks
            here = pl.ds(pl.multiple_of(piece * step, step), step)
            values = [[None, None] for _ in range(2 * shards + 1)]
            for n, slots in enumerate(sets):
                lanes = slice(n % 2 * LANES, (n % 2 + 1) * LANES)
                for p in range(2):
                    arrays = []
                    for g in range(fan):
                        at = pl.multiple_of(c1 * spread + g * rows + piece * step, step)
                        arrays.append(sums[n // 2, p, pl.ds(at, step), lanes])
                    for f, array in zip(slots, swap_lanes(arrays, width)):
                        if f is not None:
                            values[f][p] = array
            for b, value in enumerate(inverse_ladder([tuple(v) for v in values])):
                result[sig, b // 2, (b % 2) * near + c1, here, :] = value
            return carry

        for part in range(near):
            lax.fori_loop(part * chunks, (part + 1) * chunks, chunk, 0)
            for j, d in peers:

                @pl.when((c ^ d) % near == part)
                def _():
                    outcome(sig, j, d, False).start()


    flip = (
        lax.broadcasted_iota(jnp.int32, (length, length), 0)
        + lax.broadcasted_iota(jnp.int32, (length, length), 1)
        == length - 1
    )
    flip = jnp.where(flip, 1.0, 0.0).astype(jnp.bfloat16)
    first = lane_group(width) == 0
    even_lane = (lane_group(width) & 1) == 0

    def packets(real, imag):
        arrays = []
        for q in range(pack):
            arrays += [real[q * share : (q + 1) * share], imag[q * share : (q + 1) * share]]
        return swap_lanes(arrays, 2 * width)

    def members(n):
        return [n * (fan // 2) + i for i in range(fan // 2)] if n < main else []

    def post(odd, r, data):
        code, largest = encode(data)
        grads[odd, r, :share] = code
        grads[odd, r, share:] = jnp.broadcast_to(largest, (16, LANES)).astype(jnp.bfloat16)

    def send(odd, r):
        @pl.when(s != r)
        def _():
            slope(odd, r).start()

    forward(0)
    for m in range(len(couples)):
        analyse(0, m)

    own[2].wait()
    for j in range(1, shards):
        spectrum(j, True).wait_recv()

    @pl.when(s != 0)
    def _():
        extra(s).wait_recv()

    for n in range(main + 1):
        if n < main:
            arrays = swap_lanes([hheld[r] for r in members(n)], 2 * width)
            fr = jnp.concatenate(arrays[0::2], axis=0)
            fi = jnp.concatenate(arrays[1::2], axis=0)
        else:
            small = length // 4 // 2 // pack
            pieces = [[], []]
            for q in range(pack):
                for t in range(STEPS):
                    for half in range(2):
                        if t >= STEPS // 2:
                            for p in range(2):
                                pieces[p].append(jnp.zeros((small, LANES), jnp.float32))
                            continue
                        block = special[t * small : (t + 1) * small]
                        for p in range(2):
                            shift = ((q * 2 + half) * 2 + p) * width
                            moved = pltpu.roll(block, LANES - shift, 1) if shift else block
                            pieces[p].append(jnp.where(first, moved, 0.0))
            fr, fi = (jnp.concatenate(piece, axis=0) for piece in pieces)
        weight = jnp.full((1, LANES), 2.0 / total, jnp.float32)
        if 0 in sets[n]:
            weight = jnp.where(first, 1.0 / total, weight)
        lanes = slice(n % 2 * LANES, (n % 2 + 1) * LANES)
        filters[n // 2, 0, :, lanes] = fr * weight
        filters[n // 2, 1, :, lanes] = fi * weight

    for m in range(len(couples)):
        synthesise(0, m)
    inverse(0)

    arrived(1)
    forward(1)
    for n in range(main + 1):
        if n % 2 == 0:
            analyse(1, n // 2)
        lanes = slice(n % 2 * LANES, (n % 2 + 1) * LANES)
        sr, si = (spectra[0, n // 2, p, :, lanes] for p in range(2))
        cr, ci = (spectra[1, n // 2, p, :, lanes] for p in range(2))
        slope_real = (sr * cr + si * ci) * (1.0 / total)
        slope_imag = (sr * ci - si * cr) * (1.0 / total)
        if n < main:
            for r, part in zip(members(n), packets(slope_real, slope_imag)):
                post(0, r, part)
            high, low = halves(jnp.concatenate([slope_real, slope_imag], axis=1))
            turned_over = jnp.dot(flip, high, preferred_element_type=jnp.float32) + jnp.dot(
                flip, low, preferred_element_type=jnp.float32
            )
            for r, part in zip(
                members(n), packets(turned_over[:, :LANES], -turned_over[:, LANES:])
            ):
                flipped[r] = part
        else:
            last = jnp.zeros((share, LANES), jnp.float32)
            for q in range(pack):
                for p, side in enumerate((slope_real, slope_imag)):
                    place = (q * 2 + p) * 2
                    moved = side[q * share : (q + 1) * share]
                    moved = pltpu.roll(moved, place * width, 1) if place else moved
                    last = jnp.where(lane_group(width) == place, moved, last)
        if n:
            for r in members(n - 1):
                send(0, r)

    for r in range(shards):
        place = mirrored(r, bits)
        near_even = flipped[mirrored(shards - place, bits)] if place else last
        post(1, r, jnp.where(even_lane, near_even, flipped[shards - 1 - r]))

    for m in range(len(couples)):
        synthesise(1, m)
        if m == 0:
            for r in range(shards):
                send(1, r)
    mine = [
        pltpu.make_async_copy(grads.at[odd, s], landed.at[odd, s], own_sem.at[4 + odd])
        for odd in range(2)
    ]
    for copy in mine:
        copy.start()
    inverse(1)
    rest = pltpu.make_async_copy(
        result.at[:, s, c], found.at[:, c * shards + s], own_sem.at[6]
    )
    rest.start()

    tall = share // STEPS

    def gather(odd):
        mine[odd].wait()
        for r in range(shards):

            @pl.when(s != r)
            def _():
                arrival(odd, r).wait_recv()

        def piece(t, carry):
            column, piece = t // STEPS, t % STEPS
            arrays = []
            for u in range(fan):
                block = landed.at[odd, column * fan + u]
                largest = block[share : share + 16].astype(jnp.float32)[0:1]
                at = pl.ds(pl.multiple_of(piece * tall, tall), tall)
                arrays.append(decode(block[at], largest))
            for i, slope_part in enumerate(swap_lanes(arrays, width)):
                at = pl.ds(2 * tall * piece + odd, tall, stride=2)
                gathered[column, i // 2 % 2, i % 2, i // 4, at, :] = slope_part
            return carry

        lax.fori_loop(0, gathered.shape[0] * STEPS, piece, 0)

    for odd in range(2):
        gather(odd)
    stores = [
        pltpu.make_async_copy(
            gathered.at[i],
            slopes.at[:, :, :, :, pl.ds(i * LANES, LANES)],
            own_sem.at[7 + i],
        )
        for i in range(gathered.shape[0])
    ]
    for store in stores:
        store.start()

    for sig in range(2):
        for j, d in peers:
            token(sig, j, d, False).wait_send()
    for j in range(1, shards):
        spectrum(j, False).wait_send()

    @pl.when(s == 0)
    def _():
        for j in range(1, shards):
            extra(j).wait_send()

    for odd in range(2):
        for r in range(shards):

            @pl.when(s != r)
            def _():
                slope(odd, r).wait_send()

    for copy in stores + [rest]:
        copy.wait()
    for sig in range(2):
        for j, d in peers:
            outcome(sig, j, d, True).wait_recv()
        for j, d in peers:
            outcome(sig, j, d, False).wait_send()


def convolve(inputs, filt, tables, shards, groups):
    rows, channels = inputs[0].shape
    devices = shards * groups
    width = channels // devices
    fan = LANES // width
    pack = fan // 4
    short = rows // fan
    matrix, twiddle = tables
    sets, _, length, _ = twiddle.shape
    share = length // pack
    couples = (sets + 1) // 2
    raw = filt.reshape(2, 2, pack, 2 * share, filt.shape[4])
    dma, vmem = pltpu.SemaphoreType.DMA, pltpu.VMEM
    f32, bf16 = jnp.float32, jnp.bfloat16
    return pl.pallas_call(
        functools.partial(convolve_kernel, shards, groups),
        out_shape=(
            jax.ShapeDtypeStruct((2, devices, short, LANES), f32),
            jax.ShapeDtypeStruct(raw.shape, f32),
        ),
        in_specs=[ANY] * 7,
        out_specs=(ANY, ANY),
        scratch_shapes=[
            vmem((4, rows, channels), bf16),
            vmem((raw.shape[4] // LANES,) + raw.shape[:4] + (LANES,), f32),
            vmem(matrix.shape, bf16),
            vmem(twiddle.shape, f32),
            vmem((2, devices, 2, short, LANES), bf16),
            vmem((shards, share, LANES), f32),
            vmem((shards, share // 2, LANES), f32),
            vmem((2, shards, groups, 2, short, LANES), bf16),
            vmem((shards, share, LANES), f32),
            vmem((share // 4, LANES), f32),
            vmem((couples, 2 * length, 2 * LANES), bf16),
            vmem((couples, 2 * length, 2 * LANES), bf16),
            vmem((2, couples, 2, length, 2 * LANES), f32),
            vmem((couples, 2, length, 2 * LANES), f32),
            vmem((couples, 2, length, 2 * LANES), f32),
            vmem((shards, share, LANES), f32),
            vmem((2, shards, share + 16, LANES), bf16),
            vmem((2, shards, share + 16, LANES), bf16),
            vmem((raw.shape[4] // LANES,) + raw.shape[:4] + (LANES,), f32),
            vmem((2, shards, groups, short, LANES), f32),
            dma((6 + raw.shape[4] // LANES,)),
            dma((7 + raw.shape[4] // LANES,)),
            dma((2, devices)),
            dma((2, devices)),
            dma((shards,)),
            dma((shards,)),
            dma((shards,)),
            dma,
            dma((2, shards)),
            dma((2, shards)),
            dma((2, devices)),
            dma((2, devices)),
        ],
        compiler_params=pltpu.CompilerParams(
            collective_id=0, has_side_effects=True, vmem_limit_bytes=63 * 1024 * 1024
        ),
        name="convolve",
    )(*inputs, raw, matrix, twiddle)


def finish_kernel(width, fan, values, gate_in, gate_out, cotangent, found, slopes, *outs):
    rows = found.shape[2]
    outs[4][...] = slopes[...]
    for block in range(found.shape[1] // fan):
        conv, back = (
            swap_lanes([found[sig, block * fan + u] for u in range(fan)], width)
            for sig in range(2)
        )
        lanes = slice(block * LANES, (block + 1) * LANES)
        for g in range(fan):
            here = slice(g * rows, (g + 1) * rows)

            def wide(ref):
                return ref[here, lanes].astype(jnp.float32)

            outs[0][here, lanes] = (wide(gate_out) * conv[g]).astype(jnp.bfloat16)
            outs[1][here, lanes] = (back[g] * wide(gate_in)).astype(jnp.bfloat16)
            outs[2][here, lanes] = (back[g] * wide(values)).astype(jnp.bfloat16)
            outs[3][here, lanes] = (wide(cotangent) * conv[g]).astype(jnp.bfloat16)


def finish(inputs, found, slopes):
    rows, channels = inputs[0].shape
    _, devices, short, _ = found.shape
    width = channels // devices
    fan = LANES // width
    steps = 2
    tiles = channels // LANES // steps
    column = pl.BlockSpec((rows, tiles * LANES), lambda t: (0, t))
    shape = slopes.shape
    part = pl.BlockSpec(shape[:3] + (shape[3] // steps, shape[4]), lambda t: (0, 0, 0, t, 0))
    return pl.pallas_call(
        functools.partial(finish_kernel, width, fan),
        grid=(steps,),
        out_shape=tuple(jax.ShapeDtypeStruct((rows, channels), jnp.bfloat16) for _ in range(4))
        + (jax.ShapeDtypeStruct(shape, jnp.float32),),
        in_specs=[column] * 4
        + [pl.BlockSpec((2, tiles * fan, short, LANES), lambda t: (0, t, 0, 0)), part],
        out_specs=(column,) * 4 + (part,),
        name="finish",
    )(*inputs, found, slopes)


def make_tables(shards, fan, length):
    counter = np.arange(length)
    angle = 2.0 * math.pi * (np.outer(counter, counter) % length) / length
    cos, sin = np.cos(angle), np.sin(angle)
    whole = np.block([[cos, sin], [-sin, cos]])
    high = whole.astype(jnp.bfloat16)
    low = (whole - high.astype(np.float64)).astype(jnp.bfloat16)
    total = 4 * shards * length
    turns = []
    for slots in residues(shards, fan):
        lanes = np.repeat([0 if f is None else f for f in slots], LANES // fan)
        turn = 2.0 * math.pi * (counter[:, None] * lanes[None, :] % total) / total
        turns.append(np.stack([np.cos(turn), np.sin(turn)]))
    twiddle = np.stack(turns).astype(np.float32)
    return jnp.asarray(np.stack([high, low])), jnp.asarray(twiddle)


def on_device(shards, groups, values_in, gate_in, gate_out, cotangent, filter_spectra):
    inputs = (values_in, gate_in, gate_out, cotangent)
    rows, channels = values_in.shape
    fan = LANES * shards * groups // channels
    tables = make_tables(shards, fan, rows * groups // 2)
    found, slopes = convolve(inputs, filter_spectra, tables, shards, groups)
    outs = finish(inputs, found, slopes)
    return tuple(outs[:4]) + (outs[4].reshape(filter_spectra.shape),)


def solution(mesh):
    tokens = P(("seq", "chan"), None)
    spectrum = P(None, "seq", None, None, "chan")
    return jax.shard_map(
        functools.partial(on_device, mesh.shape["seq"], mesh.shape["chan"]),
        mesh=mesh,
        in_specs=(tokens, tokens, tokens, tokens, spectrum),
        out_specs=(tokens, tokens, tokens, tokens, spectrum),
        check_vma=False,
    )
```
